256 devices in a mesh: dp: 32 (over z_lo, y, x), seq: 8 (over z_hi, core).
Axes of the slice: x: 4, y: 4, z: 8 (z_hi: 4, z_lo: 2; z = z_hi * 2 + z_lo), core: 2. Of those that a mesh axis runs over, the one named last changes fastest.
Arguments:
- tokens: bfloat16 [32, 1024, 1024], P('dp', 'seq'), may hold values from -6 to 6
- positions: int32 [32, 1024], P('dp', 'seq'), may hold values from 0 to 4095
- counts: int32 [32, 8], P('dp'), may hold values from 1 to 128, 768 in all within a row
- ln_gain: float32 [1024], replicated, may hold values from 0.1 to 1.9
- w_qkv: bfloat16 [3, 1024, 1024], replicated
- w_out: bfloat16 [1024, 1024], replicated, may hold values from -0.1875 to 0.1875
- d_out: bfloat16 [32, 1024, 1024], P('dp', 'seq'), may hold values from -6 to 6
Outputs:
- d_tokens: bfloat16 [32, 1024, 1024], P('dp', 'seq')
- grad_qkv: float32 [3, 1024, 1024], P(None, 'seq', 'dp')
- grad_out: float32 [1024, 1024], P('dp', 'seq')
The draws below stay inside these ranges and needn't reach their ends.
Inputs may be any that keep to these rules, and one draw needn't show every extreme that they name: Each record's counts sum to 768, and the largest of them is 128.
All inputs are finite; a program needn't handle non-finite values.
Results may differ from the reference program's by a relative error of at most 0.0075.
Values may be sent and summed in bfloat16 or wider, within the bound.
A program may use at most 128 MiB of HBM per device.

```python
import math
import jax
import jax.numpy as jnp
import numpy as np
from jax import lax

D = 1024
HEADS = 16
HEAD_DIM = 64
CAP = 128
NPOS = 4096
SLOTS = 1024
VIS = 768
BATCH = 32
N_SEQ = 8


def draw_w_qkv(key, part):
    base = jax.random.normal(jax.random.fold_in(key, 11), (3, D, D), jnp.float32) * D ** (-0.5)
    return base.astype(jnp.bfloat16)


def with_ends(values, own_key, low, high):
    extent = values.shape
    spot = [jax.random.randint(jax.random.fold_in(own_key, axis), (), 0, extent[axis]) for axis in range(len(extent))]
    values = values.at[tuple(spot)].set(low)
    longest = extent.index(max(extent))
    spot[longest] = (spot[longest] + 1) % extent[longest]
    return values.at[tuple(spot)].set(high)


def shard_levels(stream_key, extent, split, least, largest):
    loudness = 1.0
    for dim, shards_of in split:
        heights = jax.random.uniform(jax.random.fold_in(jax.random.fold_in(stream_key, 6), dim), (shards_of,), jnp.float32, least / len(split), largest / len(split))
        loudness = loudness * jnp.repeat(jnp.exp(heights), extent[dim] // shards_of).reshape((-1,) + (1,) * (len(extent) - 1 - dim))
    return loudness


def profile(number_of, total, bound, skew):
    loads = [(1 << 20) // math.isqrt(rank ** skew) + 1 for rank in range(2, number_of + 1)]
    spare, holding = total - bound - (number_of - 1), [1] * (number_of - 1)
    while spare > 0:
        candidates = [i for i in range(number_of - 1) if holding[i] < bound]
        whole, budget = sum([loads[i] for i in candidates]), spare
        for i in candidates:
            more = min(bound - holding[i], max(1, budget * loads[i] // whole), spare)
            holding[i] = holding[i] + more
            spare = spare - more
    return np.array([bound] + holding)


def ragged_sizes(rng, amount, total, most, lean):
    if amount == 2:
        one = jax.random.randint(rng, (), max(1, total - most), min(most, total - 1) + 1)
        return jnp.stack([one, total - one])
    sizes = jnp.asarray(profile(amount, total, most, lean), jnp.int32)
    twos = (amount - 1) // 2
    donor, receiver = sizes[1:1 + 2 * twos:2], sizes[2:2 + 2 * twos:2]
    room = jnp.minimum(donor - 1, most - receiver)
    moved = jax.random.randint(jax.random.fold_in(rng, 1), (twos,), 0, 1 << 20) % (room + 1)
    sizes = sizes.at[1:1 + 2 * twos:2].set(donor - moved).at[2:2 + 2 * twos:2].set(receiver + moved)
    return sizes[jax.random.permutation(jax.random.fold_in(rng, 2), amount)]


def noise(own_key, dims, width, most, split=(), held_as=jnp.bfloat16):
    gain = shard_levels(own_key, dims, split, -0.22, 0.18) if split else 1.0
    entries = jax.random.normal(own_key, dims, jnp.float32) * width * gain
    return jnp.minimum(jnp.maximum(entries, -most), most).astype(held_as)


def setup_inputs(seed: int = 0) -> dict:
    arg_keys = jax.random.split(jax.random.key(seed), 8)
    tokens = noise(arg_keys[0], (BATCH, SLOTS, D), 1.0, 6.0, ((0, 32), (1, 8)))
    positions = with_ends(jax.random.randint(arg_keys[1], (BATCH, SLOTS), 0, NPOS), jax.random.fold_in(arg_keys[1], 1), 0, NPOS - 1).astype(jnp.int32)
    counts = jax.vmap(lambda own: ragged_sizes(own, N_SEQ, VIS, CAP, 2))(jax.random.split(arg_keys[2], BATCH)).reshape((BATCH, N_SEQ)).astype(jnp.int32)
    ln_gain = jnp.clip(1.0 + 0.18 * jax.random.normal(arg_keys[3], (D,), jnp.float32), 0.1, 1.9)
    w_qkv = draw_w_qkv(jax.random.fold_in(arg_keys[7], 71), 0)
    w_out = noise(arg_keys[5], (D, D), D ** -0.5, 0.1875)
    d_out = noise(arg_keys[6], (BATCH, SLOTS, D), 1.0, 6.0, ((0, 32), (1, 8)))
    return {"tokens": tokens, "positions": positions, "counts": counts, "ln_gain": ln_gain, "w_qkv": w_qkv, "w_out": w_out, "d_out": d_out}


EPSILON = 1e-06
MASKED = -1e+30

def position_code(places, feature_width):
    half = feature_width // 2
    freqs = jnp.exp(jnp.arange(half, dtype=jnp.float32) * (-math.log(10000.0) / half))
    angle = places.astype(jnp.float32)[:, None] * freqs[None, :]
    return jnp.concatenate([jnp.sin(angle), jnp.cos(angle)], axis=1)

def layer_norm(inputs, places, ln_gain):
    shifted = inputs.astype(jnp.float32) + position_code(places, inputs.shape[1])
    centred = shifted - lax.optimization_barrier(jnp.mean(shifted, axis=1, keepdims=True))
    inv_std = lax.rsqrt(lax.optimization_barrier(jnp.mean(centred * centred, axis=1, keepdims=True)) + EPSILON)
    standard = centred * inv_std
    normed = (standard * ln_gain.astype(jnp.float32)).astype(jnp.bfloat16)
    return (normed, standard, inv_std)

def input_grad(query_grad, key_grad, value_grad, masked_grad, w_qkv, standard, inv_std, ln_gain):
    normed_grad = jnp.dot(query_grad, w_qkv[0], preferred_element_type=jnp.float32)
    normed_grad = normed_grad + jnp.dot(key_grad, w_qkv[1], preferred_element_type=jnp.float32)
    normed_grad = normed_grad + jnp.dot(value_grad, w_qkv[2], preferred_element_type=jnp.float32)
    unit_grad = normed_grad * ln_gain.astype(jnp.float32)
    inner = unit_grad - lax.optimization_barrier(jnp.mean(unit_grad, axis=1, keepdims=True))
    inner = inner - standard * lax.optimization_barrier(jnp.mean(unit_grad * standard, axis=1, keepdims=True))
    return (masked_grad.astype(jnp.float32) + inv_std * inner).astype(jnp.bfloat16)

def head_attention(queries, key_rows, value_rows, attn_grad, key_valid, score_scale):
    scores = jnp.dot(queries, key_rows.T, preferred_element_type=jnp.float32) * score_scale
    scores = jnp.where(key_valid[None, :], scores, MASKED)
    peak = lax.optimization_barrier(jnp.max(scores, axis=1, keepdims=True))
    expo = jnp.exp(scores - peak)
    probs = expo / lax.optimization_barrier(jnp.sum(expo, axis=1, keepdims=True))
    probs_low = probs.astype(jnp.bfloat16)
    attended = jnp.dot(probs_low, value_rows, preferred_element_type=jnp.float32)
    delta = lax.optimization_barrier(jnp.sum(attn_grad.astype(jnp.float32) * attended, axis=1))
    prob_grad = jnp.dot(attn_grad, value_rows.T, preferred_element_type=jnp.float32)
    score_grad = (probs * (prob_grad - delta[:, None])).astype(jnp.bfloat16)
    query_grad = (jnp.dot(score_grad, key_rows, preferred_element_type=jnp.float32) * score_scale).astype(jnp.bfloat16)
    key_grad = (jnp.dot(score_grad.T, queries, preferred_element_type=jnp.float32) * score_scale).astype(jnp.bfloat16)
    value_grad = jnp.dot(probs_low.T, attn_grad, preferred_element_type=jnp.float32).astype(jnp.bfloat16)
    return (attended.astype(jnp.bfloat16), query_grad, key_grad, value_grad)

def reference(tokens, positions, counts, ln_gain, w_qkv, w_out, d_out):
    score_scale = HEAD_DIM ** (-0.5)
    slot_index = jnp.arange(SLOTS, dtype=jnp.int32)

    def split_heads(array):
        return array.reshape(SLOTS, HEADS, HEAD_DIM).transpose(1, 0, 2)

    def join_heads(array):
        return array.transpose(1, 0, 2).reshape(SLOTS, D)

    def project(normed, weight):
        return jnp.dot(normed, weight.T, preferred_element_type=jnp.float32).astype(jnp.bfloat16)

    def one_record(carry, item):
        inputs, places, shard_counts, upstream = item
        valid = slot_index % CAP < jnp.repeat(shard_counts, CAP)
        normed, standard, inv_std = layer_norm(inputs, places, ln_gain)
        masked_grad = jnp.where(valid[:, None], upstream, jnp.zeros_like(upstream))
        queries = project(normed, w_qkv[0])
        key_rows = project(normed, w_qkv[1])
        value_rows = project(normed, w_qkv[2])
        attn_grad = jnp.dot(masked_grad, w_out, preferred_element_type=jnp.float32).astype(jnp.bfloat16)

        def per_head(parts):
            return head_attention(parts[0], parts[1], parts[2], parts[3], valid, score_scale)
        results = lax.map(per_head, (split_heads(queries), split_heads(key_rows), split_heads(value_rows), split_heads(attn_grad)))
        attended = join_heads(results[0])
        query_grad = join_heads(results[1])
        key_grad = join_heads(results[2])
        value_grad = join_heads(results[3])
        d_inputs = input_grad(query_grad, key_grad, value_grad, masked_grad, w_qkv, standard, inv_std, ln_gain)
        term_qkv = jnp.stack([jnp.dot(query_grad.T, normed, preferred_element_type=jnp.float32), jnp.dot(key_grad.T, normed, preferred_element_type=jnp.float32), jnp.dot(value_grad.T, normed, preferred_element_type=jnp.float32)])
        term_out = jnp.dot(masked_grad.T, attended, preferred_element_type=jnp.float32)
        return ((carry[0] + term_qkv, carry[1] + term_out), d_inputs)
    start = (jnp.zeros((3, D, D), jnp.float32), jnp.zeros((D, D), jnp.float32))
    sums, d_tokens = lax.scan(one_record, start, (tokens, positions, counts, d_out))
    factor = 1.0 / math.sqrt(BATCH * VIS)
    return (d_tokens, sums[0] * factor, sums[1] * factor)
```

```python
import math

import jax
import jax.numpy as jnp
from jax import lax
from jax.experimental import pallas as pl
from jax.experimental.pallas import tpu as pltpu
from jax.sharding import PartitionSpec as P

HEAD_DIM = 64
EPSILON = 1e-06
MASKED = -1e30
F32 = jnp.float32
BF16 = jnp.bfloat16
MESH = pl.DeviceIdType.MESH
QUERY_BLOCK = 256


def position_code(places, feature_width):
    half = feature_width // 2
    freqs = jnp.exp(jnp.arange(half, dtype=jnp.float32) * (-math.log(10000.0) / half))
    angle = places.astype(jnp.float32)[:, None] * freqs[None, :]
    return jnp.concatenate([jnp.sin(angle), jnp.cos(angle)], axis=1)


def layer_norm(inputs, places, ln_gain):
    shifted = inputs.astype(jnp.float32) + position_code(places, inputs.shape[1])
    centred = shifted - jnp.mean(shifted, axis=1, keepdims=True)
    inv_std = lax.rsqrt(jnp.mean(centred * centred, axis=1, keepdims=True) + EPSILON)
    standard = centred * inv_std
    normed = (standard * ln_gain).astype(jnp.bfloat16)
    return (normed, standard, inv_std)


def dot(left, right, left_dim, right_dim):
    return lax.dot_general(
        left, right, (((left_dim,), (right_dim,)), ((), ())), preferred_element_type=F32
    )


def turned(block):
    return block.astype(F32).T.astype(BF16)


def block_kernel(
    factor,
    normed_ref,
    masked_ref,
    standard_ref,
    inv_ref,
    gain_ref,
    bias_ref,
    w_qkv_ref,
    w_out_ref,
    d_tokens_ref,
    sums_ref,
    all_normed,
    all_masked,
    normed_t,
    masked_t,
    weights,
    out_weights,
    query,
    key,
    value,
    grad,
    query_t,
    key_grad_t,
    value_grad_t,
    grads,
    attended,
    returned,
    relayed,
    pieces,
    pieces_in,
    half_out,
    half_in,
    total,
    load_sem,
    gather_send,
    gather_recv,
    back_send,
    back_recv,
    sum_send,
    sum_recv,
):
    me = lax.axis_index("seq")
    place = lax.axis_index("dp")
    chip, core = me // 2, me % 2
    ahead, behind, across = (chip + 1) % 4, (chip + 3) % 4, (chip + 2) % 4
    twin = 1 - core
    after, before, far, mate = (
        ahead * 2 + core,
        behind * 2 + core,
        across * 2 + core,
        chip * 2 + twin,
    )
    after_twin, before_twin, far_twin = ahead * 2 + twin, behind * 2 + twin, across * 2 + twin
    layer, spot = place // 16, place % 16

    loads = [
        pltpu.make_async_copy(w_qkv_ref, weights, load_sem.at[0]),
        pltpu.make_async_copy(
            w_out_ref.at[:, pl.ds(pl.multiple_of(me * 128, 128), 128)], out_weights, load_sem.at[1]
        ),
        pltpu.make_async_copy(masked_ref, all_masked.at[me], load_sem.at[2]),
        pltpu.make_async_copy(normed_ref, all_normed.at[me], load_sem.at[3]),
    ]
    for load in loads:
        load.start()

    barrier = pltpu.get_barrier_semaphore()
    for step in range(1, 8):
        pl.semaphore_signal(
            barrier, inc=1, device_id={"seq": (me + step) % 8}, device_id_type=MESH
        )
    for step in range(1, 16):
        pl.semaphore_signal(
            barrier, inc=1, device_id={"dp": layer * 16 + (spot + step) % 16}, device_id_type=MESH
        )
    other_layer = (1 - layer) * 16 + spot
    pl.semaphore_signal(barrier, inc=1, device_id={"dp": other_layer}, device_id_type=MESH)
    pl.semaphore_wait(barrier, 23)

    def gather(index, source, target, device):
        return pltpu.make_async_remote_copy(
            src_ref=source,
            dst_ref=target,
            send_sem=gather_send.at[index],
            recv_sem=gather_recv.at[index],
            device_id={"seq": device},
            device_id_type=MESH,
        )

    started = []

    def go(copy):
        copy.start()
        started.append(copy)

    for base, own, full in ((0, masked_ref, all_masked), (13, normed_ref, all_normed)):
        go(gather(base + 0, own.at[0], full.at[me, 0], after))
        go(gather(base + 1, own.at[1], full.at[me, 1], before))
        go(gather(base + 2, own.at[1], full.at[me, 1], after))
        go(gather(base + 3, own.at[0], full.at[me, 0], before))
        go(gather(base + 4, own, full.at[me], mate))

    def landed(index, full, *spot_):
        view = full.at[spot_]
        gather(index, view, view, mate).wait_recv()

    def relay_near(base, full):
        landed(base + 0, full, before, 0)
        go(gather(base + 5, full.at[before, 0], full.at[before, 0], after))
        go(gather(base + 7, full.at[before, 0], full.at[before, 0], mate))
        landed(base + 1, full, after, 1)
        go(gather(base + 6, full.at[after, 1], full.at[after, 1], before))
        go(gather(base + 8, full.at[after, 1], full.at[after, 1], mate))
        landed(base + 2, full, before, 1)
        go(gather(base + 9, full.at[before, 1], full.at[before, 1], mate))
        landed(base + 3, full, after, 0)
        go(gather(base + 10, full.at[after, 0], full.at[after, 0], mate))

    def relay_far(base, full):
        landed(base + 5, full, far, 0)
        go(gather(base + 11, full.at[far, 0], full.at[far, 0], mate))
        landed(base + 6, full, far, 1)
        go(gather(base + 12, full.at[far, 1], full.at[far, 1], mate))

    def near_twin(base, full):
        landed(base + 4, full, mate)
        landed(base + 7, full, before_twin, 0)
        landed(base + 8, full, after_twin, 1)
        landed(base + 9, full, before_twin, 1)
        landed(base + 10, full, after_twin, 0)

    def far_twin_(base, full):
        landed(base + 11, full, far_twin, 0)
        landed(base + 12, full, far_twin, 1)

    def rows_of(which):
        return pl.ds(pl.multiple_of(which * 256, 256), 256)

    def project_masked(which):
        rows = rows_of(which)
        block = all_masked[pl.ds(which * 2, 2)].reshape(256, 1024)
        grad[rows, :] = dot(block, out_weights[...], 1, 0).astype(BF16)
        masked_t[:, rows] = turned(block)

    def project_normed(which):
        rows = rows_of(which)
        block = all_normed[pl.ds(which * 2, 2)].reshape(256, 1024)
        heads = pl.ds(pl.multiple_of(me * 128, 128), 128)
        queries = dot(block, weights[0, heads, :], 1, 1).astype(BF16).astype(F32) * 0.125
        query[rows, :] = queries.astype(BF16)
        query_t[:, rows] = queries.T.astype(BF16)
        key[rows, :] = dot(block, weights[1, heads, :], 1, 1).astype(BF16)
        value[rows, :] = dot(block, weights[2, heads, :], 1, 1).astype(BF16)
        normed_t[:, rows] = turned(block)

    for load in loads:
        load.wait()
    relay_near(0, all_masked)
    near_twin(0, all_masked)

    def near_masked(step, carry):
        project_masked((chip + 3 + step) % 4)
        return carry

    lax.fori_loop(0, 3, near_masked, 0)
    relay_near(13, all_normed)
    near_twin(13, all_normed)

    def near_normed(step, carry):
        project_normed((chip + 3 + step) % 4)
        return carry

    lax.fori_loop(0, 3, near_normed, 0)
    relay_far(0, all_masked)
    far_twin_(0, all_masked)
    project_masked(across)
    relay_far(13, all_normed)
    far_twin_(13, all_normed)
    project_normed(across)

    key_grad_t[...] = jnp.zeros_like(key_grad_t)
    value_grad_t[...] = jnp.zeros_like(value_grad_t)

    def attend(step, carry):
        rows = pl.ds(pl.multiple_of(step * QUERY_BLOCK, QUERY_BLOCK), QUERY_BLOCK)
        bias = bias_ref[...]
        for head in range(2):
            span = slice(head * HEAD_DIM, (head + 1) * HEAD_DIM)
            scores = dot(query[rows, span], key[:, span], 1, 1) + bias
            peak = jnp.max(scores, axis=1, keepdims=True)
            expo = jnp.exp(scores - peak)
            share = 1.0 / jnp.sum(expo, axis=1, keepdims=True)
            expo_low = expo.astype(BF16)
            mixed = dot(expo_low, value[:, span], 1, 0) * share
            scaled = grad[rows, span].astype(F32) * share
            delta = jnp.sum(mixed * scaled, axis=1, keepdims=True)
            prob_grad = dot(scaled.astype(BF16), value[:, span], 1, 1)
            score_grad = (expo * (prob_grad - delta)).astype(BF16)
            attended[rows, span] = mixed.astype(BF16)
            grads[rows, span] = (dot(score_grad, key[:, span], 1, 0) * 0.125).astype(BF16)
            key_grad_t[span, :] += dot(query_t[span, rows], score_grad, 1, 0)
            value_grad_t[span, :] += dot(scaled.T.astype(BF16), expo_low, 1, 0)
        return carry

    lax.fori_loop(0, 1024 // QUERY_BLOCK, attend, 0)
    grads[:, 128:256] = key_grad_t[...].T.astype(BF16)
    grads[:, 256:384] = value_grad_t[...].T.astype(BF16)

    def back(index, source, target, device):
        return pltpu.make_async_remote_copy(
            src_ref=source,
            dst_ref=target,
            send_sem=back_send.at[index],
            recv_sem=back_recv.at[index],
            device_id={"seq": device},
            device_id_type=MESH,
        )

    def slots(which):
        return grads.at[pl.ds(pl.multiple_of(which * 128, 128), 128), :]

    go(back(0, slots(far), relayed.at[0], after))
    go(back(1, slots(far_twin), relayed.at[1], before))
    go(back(2, slots(after), returned.at[me], after))
    go(back(3, slots(after_twin), returned.at[me], after_twin))
    go(back(4, slots(before), returned.at[me], before))
    go(back(5, slots(before_twin), returned.at[me], before_twin))
    go(back(6, slots(mate), returned.at[me], mate))

    pieces[:, :, :, :384] = dot(normed_t[...], grads[...], 1, 0).astype(BF16).reshape(2, 16, 32, 384)
    pieces[:, :, :, 384:] = (
        dot(masked_t[...], attended[...], 1, 0).astype(BF16).reshape(2, 16, 32, 128)
    )

    def scatter(step, source, target, device):
        return pltpu.make_async_remote_copy(
            src_ref=source,
            dst_ref=target,
            send_sem=sum_send.at[step],
            recv_sem=sum_recv.at[step],
            device_id={"dp": device},
            device_id_type=MESH,
        )

    for step in range(1, 16):
        to = (spot + step) % 16
        go(scatter(step, pieces.at[:, to], pieces_in.at[spot], layer * 16 + to))

    back(0, relayed.at[0], relayed.at[0], mate).wait_recv()
    go(back(7, relayed.at[0], returned.at[before], after))
    back(1, relayed.at[1], relayed.at[1], mate).wait_recv()
    go(back(8, relayed.at[1], returned.at[after], before_twin))

    def add_rows(which, block, first=False):
        heads = pl.ds(pl.multiple_of(which * 128, 128), 128)
        term = dot(block[:, :128], weights[0, heads, :], 1, 0)
        term = term + dot(block[:, 128:256], weights[1, heads, :], 1, 0)
        term = term + dot(block[:, 256:], weights[2, heads, :], 1, 0)
        total[...] = term if first else total[...] + term

    def came(index, which):
        back(index, returned.at[which], returned.at[which], mate).wait_recv()
        add_rows(which, returned[which])

    add_rows(me, grads[pl.ds(pl.multiple_of(me * 128, 128), 128), :], True)
    came(6, mate)
    came(2, before)
    came(3, before_twin)
    came(4, after)
    came(5, after_twin)

    for step in range(1, 16):
        view = pieces_in.at[(spot + 16 - step) % 16]
        scatter(step, view, view, other_layer).wait_recv()
    summed = pieces[:, spot].astype(F32)
    for step in range(1, 16):
        summed = summed + pieces_in[(spot + step) % 16].astype(F32)
    pieces_in[spot] = summed.astype(BF16)
    last = scatter(0, pieces_in.at[spot, 1 - layer], half_in, other_layer)
    go(last)

    came(7, far)
    came(8, far_twin)
    unit_grad = total[...] * gain_ref[...]
    standard = standard_ref[...]
    inner = unit_grad - jnp.mean(unit_grad, axis=1, keepdims=True)
    inner = inner - standard * jnp.mean(unit_grad * standard, axis=1, keepdims=True)
    own_masked = masked_ref[...].reshape(128, 1024).astype(F32)
    d_tokens_ref[...] = (own_masked + inv_ref[...] * inner).astype(BF16)

    last.wait_recv()
    half = jnp.where(layer == 0, summed[0], summed[1])
    sums_ref[...] = (half + half_in[...].astype(F32)) * factor
    for copy in started:
        copy.wait_send()


def shards(tokens, positions, counts, ln_gain, w_qkv, w_out, d_out):
    inputs = tokens[0]
    upstream = d_out[0]
    capacity, feature_width = inputs.shape
    shard_total = lax.axis_size("seq")
    shard_index = lax.axis_index("seq")
    slot_count = capacity * shard_total
    key_valid = jnp.arange(slot_count, dtype=jnp.int32) % capacity < jnp.repeat(counts[0], capacity)
    own_valid = lax.dynamic_slice_in_dim(key_valid, shard_index * capacity, capacity)
    normed, standard, inv_std = layer_norm(inputs, positions[0], ln_gain)
    masked = jnp.where(own_valid[:, None], upstream, jnp.zeros_like(upstream))
    bias = jnp.where(key_valid, 0.0, MASKED).astype(F32)[None, :]
    factor = 1.0 / math.sqrt(lax.axis_size("dp") * (3 * slot_count // 4))
    vmem = pl.BlockSpec(memory_space=pltpu.VMEM)
    anywhere = pl.BlockSpec(memory_space=pl.ANY)
    d_tokens, sums = pl.pallas_call(
        lambda *refs: block_kernel(factor, *refs),
        out_shape=(
            jax.ShapeDtypeStruct((128, 1024), BF16),
            jax.ShapeDtypeStruct((32, 512), F32),
        ),
        in_specs=[vmem] * 6 + [anywhere] * 2,
        out_specs=(vmem, vmem),
        scratch_shapes=[
            pltpu.VMEM((8, 2, 64, 1024), BF16),
            pltpu.VMEM((8, 2, 64, 1024), BF16),
            pltpu.VMEM((1024, 1024), BF16),
            pltpu.VMEM((1024, 1024), BF16),
            pltpu.VMEM((3, 1024, 1024), BF16),
            pltpu.VMEM((1024, 128), BF16),
            pltpu.VMEM((1024, 128), BF16),
            pltpu.VMEM((1024, 128), BF16),
            pltpu.VMEM((1024, 128), BF16),
            pltpu.VMEM((1024, 128), BF16),
            pltpu.VMEM((128, 1024), BF16),
            pltpu.VMEM((128, 1024), F32),
            pltpu.VMEM((128, 1024), F32),
            pltpu.VMEM((1024, 384), BF16),
            pltpu.VMEM((1024, 128), BF16),
            pltpu.VMEM((8, 128, 384), BF16),
            pltpu.VMEM((2, 128, 384), BF16),
            pltpu.VMEM((2, 16, 32, 512), BF16),
            pltpu.VMEM((16, 2, 32, 512), BF16),
            pltpu.VMEM((32, 512), BF16),
            pltpu.VMEM((32, 512), BF16),
            pltpu.VMEM((128, 1024), F32),
            pltpu.SemaphoreType.DMA((4,)),
            pltpu.SemaphoreType.DMA((26,)),
            pltpu.SemaphoreType.DMA((26,)),
            pltpu.SemaphoreType.DMA((9,)),
            pltpu.SemaphoreType.DMA((9,)),
            pltpu.SemaphoreType.DMA((16,)),
            pltpu.SemaphoreType.DMA((16,)),
        ],
        compiler_params=pltpu.CompilerParams(
            collective_id=0, has_side_effects=True, vmem_limit_bytes=60 * 1024 * 1024
        ),
        name="attention_block_grads",
    )(
        normed.reshape(2, 64, 1024),
        masked.reshape(2, 64, 1024),
        standard,
        inv_std,
        ln_gain[None, :],
        bias,
        w_qkv,
        w_out,
    )
    grad_qkv = jnp.transpose(sums[:, :384].reshape(32, 3, 128), (1, 2, 0))
    return (d_tokens[None], grad_qkv, sums[:, 384:])


def solution(mesh):
    placed = (
        P("dp", "seq", None),
        P("dp", "seq"),
        P("dp", None),
        P(),
        P(),
        P(),
        P("dp", "seq", None),
    )
    return jax.shard_map(
        shards,
        mesh=mesh,
        in_specs=placed,
        out_specs=(P("dp", "seq", None), P(None, "seq", "dp"), P("dp", "seq")),
        check_vma=False,
    )
```

```python
import math

import jax
import jax.numpy as jnp
from jax import lax
from jax.experimental import pallas as pl
from jax.experimental.pallas import tpu as pltpu
from jax.sharding import PartitionSpec as P

HEAD_DIM = 64
EPSILON = 1e-06
MASKED = -1e30
F32 = jnp.float32
BF16 = jnp.bfloat16
MESH = pl.DeviceIdType.MESH
QUERY_BLOCK = 256


def sin_cos(angle):
    turns = jnp.floor(angle * (2.0 / math.pi) + 0.5)
    rest = angle - turns * 1.5703125
    rest = rest - turns * 4.837512969970703125e-4
    rest = rest - turns * 7.54978995489188216e-8
    square = rest * rest
    sine = rest + rest * square * (
        -1.6666654611e-1 + square * (8.3321608736e-3 - square * 1.9515295891e-4)
    )
    cosine = (
        1.0
        - 0.5 * square
        + square
        * square
        * (4.166664568298827e-2 + square * (-1.388731625493765e-3 + square * 2.443315711809948e-5))
    )
    quarter = turns - 4.0 * jnp.floor(turns * 0.25)
    odd = (quarter == 1.0) | (quarter == 3.0)
    sine, cosine = jnp.where(odd, cosine, sine), jnp.where(odd, sine, cosine)
    sine = jnp.where(quarter >= 2.0, -sine, sine)
    cosine = jnp.where((quarter == 1.0) | (quarter == 2.0), -cosine, cosine)
    return sine, cosine


def dot(left, right, left_dim, right_dim):
    return lax.dot_general(
        left, right, (((left_dim,), (right_dim,)), ((), ())), preferred_element_type=F32
    )


def turned(block):
    return block.astype(F32).T.astype(BF16)


def block_kernel(
    factor,
    tokens_ref,
    d_out_ref,
    positions_ref,
    counts_ref,
    gain_ref,
    w_qkv_ref,
    w_out_ref,
    d_tokens_ref,
    sums_ref,
    normed_ref,
    masked_ref,
    standard_ref,
    inv_ref,
    bias_ref,
    expos,
    mixes,
    shares,
    all_normed,
    all_masked,
    normed_t,
    masked_t,
    weights,
    out_weights,
    query,
    key,
    value,
    grad,
    query_t,
    key_grad_t,
    value_grad_t,
    grads,
    attended,
    returned,
    relayed,
    out_part,
    pieces,
    row_in,
    column_in,
    row_low,
    column_low,
    row_end,
    column_end,
    out_pieces,
    out_pieces_in,
    half_out,
    half_in,
    total,
    load_sem,
    gather_send,
    gather_recv,
    back_send,
    back_recv,
    sum_send,
    sum_recv,
):
    me = lax.axis_index("seq")
    place = lax.axis_index("dp")
    chip, core = me // 2, me % 2
    ahead, behind, across = (chip + 1) % 4, (chip + 3) % 4, (chip + 2) % 4
    twin = 1 - core
    after, before, far, mate = (
        ahead * 2 + core,
        behind * 2 + core,
        across * 2 + core,
        chip * 2 + twin,
    )
    after_twin, before_twin, far_twin = ahead * 2 + twin, behind * 2 + twin, across * 2 + twin
    layer, spot = place // 16, place % 16

    loads = [
        pltpu.make_async_copy(w_qkv_ref, weights, load_sem.at[0]),
        pltpu.make_async_copy(
            w_out_ref.at[:, pl.ds(pl.multiple_of(me * 128, 128), 128)], out_weights, load_sem.at[1]
        ),
    ]
    for load in loads:
        load.start()

    barrier = pltpu.get_barrier_semaphore()
    for step in range(1, 8):
        pl.semaphore_signal(
            barrier, inc=1, device_id={"seq": (me + step) % 8}, device_id_type=MESH
        )
    for step in range(1, 16):
        pl.semaphore_signal(
            barrier, inc=1, device_id={"dp": layer * 16 + (spot + step) % 16}, device_id_type=MESH
        )
    other_layer = (1 - layer) * 16 + spot
    pl.semaphore_signal(barrier, inc=1, device_id={"dp": other_layer}, device_id_type=MESH)

    slot = lax.broadcasted_iota(jnp.int32, (1, 128), 1)
    for part in range(8):
        bias_ref[:, part * 128 : (part + 1) * 128] = jnp.where(
            slot < counts_ref[0, part], 0.0, MASKED
        )
    row = lax.broadcasted_iota(jnp.int32, (128, 128), 0)
    lane = lax.broadcasted_iota(jnp.int32, (128, 128), 1)
    places = jnp.sum(
        jnp.where(row == lane, positions_ref[...].astype(F32), 0.0), axis=1, keepdims=True
    )
    freqs = jnp.exp(
        lax.broadcasted_iota(jnp.int32, (1, 512), 1).astype(F32) * (-math.log(10000.0) / 512)
    )
    own_count = counts_ref[0, me]
    for part in range(4):
        rows = slice(part * 32, (part + 1) * 32)
        sine, cosine = sin_cos(places[rows] * freqs)
        shifted = tokens_ref[rows, :].astype(F32) + jnp.concatenate([sine, cosine], axis=1)
        centred = shifted - jnp.mean(shifted, axis=1, keepdims=True)
        inv_std = lax.rsqrt(jnp.mean(centred * centred, axis=1, keepdims=True) + EPSILON)
        unit = centred * inv_std
        standard_ref[rows, :] = unit
        inv_ref[rows, :] = inv_std
        within = slice((part % 2) * 32, (part % 2) * 32 + 32)
        normed_ref[part // 2, within, :] = (unit * gain_ref[...]).astype(BF16)
        upstream = d_out_ref[rows, :]
        spots = lax.broadcasted_iota(jnp.int32, (32, 1024), 0) + part * 32
        masked_ref[part // 2, within, :] = jnp.where(
            spots < own_count, upstream.astype(F32), 0.0
        ).astype(BF16)
    all_normed[me] = normed_ref[...]
    all_masked[me] = masked_ref[...]
    pl.semaphore_wait(barrier, 23)

    def gather(index, source, target, device):
        return pltpu.make_async_remote_copy(
            src_ref=source,
            dst_ref=target,
            send_sem=gather_send.at[index],
            recv_sem=gather_recv.at[index],
            device_id={"seq": device},
            device_id_type=MESH,
        )

    started = []

    def go(copy):
        copy.start()
        started.append(copy)

    def send_own(base, own, full):
        go(gather(base + 0, own.at[0], full.at[me, 0], after))
        go(gather(base + 1, own.at[1], full.at[me, 1], before))
        go(gather(base + 2, own.at[1], full.at[me, 1], after))
        go(gather(base + 3, own.at[0], full.at[me, 0], before))
        go(gather(base + 4, own, full.at[me], mate))

    def landed(index, full, *spot_):
        view = full.at[spot_]
        gather(index, view, view, mate).wait_recv()

    def relay_first(base, full):
        landed(base + 0, full, before, 0)
        go(gather(base + 5, full.at[before, 0], full.at[before, 0], after))
        go(gather(base + 7, full.at[before, 0], full.at[before, 0], mate))
        landed(base + 1, full, after, 1)
        go(gather(base + 6, full.at[after, 1], full.at[after, 1], before))
        go(gather(base + 8, full.at[after, 1], full.at[after, 1], mate))

    def relay_second(base, full):
        landed(base + 2, full, before, 1)
        go(gather(base + 9, full.at[before, 1], full.at[before, 1], mate))
        landed(base + 3, full, after, 0)
        go(gather(base + 10, full.at[after, 0], full.at[after, 0], mate))

    def relay_far(base, full):
        landed(base + 5, full, far, 0)
        go(gather(base + 11, full.at[far, 0], full.at[far, 0], mate))
        landed(base + 6, full, far, 1)
        go(gather(base + 12, full.at[far, 1], full.at[far, 1], mate))

    upper, lower = slice(0, 32), slice(32, 64)

    def relay_first_fine(base, full):
        landed(base + 0, full, before, 0)
        go(gather(base + 5, full.at[before, 0, upper], full.at[before, 0, upper], after))
        go(gather(26, full.at[before, 0, lower], full.at[before, 0, lower], after))
        go(gather(base + 7, full.at[before, 0], full.at[before, 0], mate))
        landed(base + 1, full, after, 1)
        go(gather(base + 6, full.at[after, 1, upper], full.at[after, 1, upper], before))
        go(gather(27, full.at[after, 1, lower], full.at[after, 1, lower], before))
        go(gather(base + 8, full.at[after, 1], full.at[after, 1], mate))

    def relay_far_fine(base, full):
        landed(base + 5, full, far, 0, upper)
        go(gather(base + 11, full.at[far, 0, upper], full.at[far, 0, upper], mate))
        landed(base + 6, full, far, 1, upper)
        go(gather(base + 12, full.at[far, 1, upper], full.at[far, 1, upper], mate))
        landed(26, full, far, 0, lower)
        go(gather(28, full.at[far, 0, lower], full.at[far, 0, lower], mate))
        landed(27, full, far, 1, lower)
        go(gather(29, full.at[far, 1, lower], full.at[far, 1, lower], mate))

    def far_twin_fine(base, full):
        landed(base + 11, full, far_twin, 0, upper)
        landed(base + 12, full, far_twin, 1, upper)
        landed(28, full, far_twin, 0, lower)
        landed(29, full, far_twin, 1, lower)

    def near_twin(base, full):
        landed(base + 4, full, mate)
        landed(base + 7, full, before_twin, 0)
        landed(base + 8, full, after_twin, 1)
        landed(base + 9, full, before_twin, 1)
        landed(base + 10, full, after_twin, 0)

    def far_twin_(base, full):
        landed(base + 11, full, far_twin, 0)
        landed(base + 12, full, far_twin, 1)

    def rows_of(which):
        return pl.ds(pl.multiple_of(which * 256, 256), 256)

    def project_masked(which):
        rows = rows_of(which)
        block = all_masked[pl.ds(which * 2, 2)].reshape(256, 1024)
        grad[rows, :] = dot(block, out_weights[...], 1, 0).astype(BF16)

    def add_out_terms(which):
        rows = rows_of(which)
        block = all_masked[pl.ds(which * 2, 2)].reshape(256, 1024)
        masked_t[...] = turned(block)
        out_part[...] += dot(masked_t[...], attended[rows, :], 1, 0)

    def project_normed(which):
        rows = rows_of(which)
        block = all_normed[pl.ds(which * 2, 2)].reshape(256, 1024)
        heads = pl.ds(pl.multiple_of(me * 128, 128), 128)
        queries = dot(block, weights[0, heads, :], 1, 1).astype(BF16).astype(F32) * 0.125
        query[rows, :] = queries.astype(BF16)
        query_t[:, rows] = queries.T.astype(BF16)
        key[rows, :] = dot(block, weights[1, heads, :], 1, 1).astype(BF16)
        value[rows, :] = dot(block, weights[2, heads, :], 1, 1).astype(BF16)
        normed_t[:, rows] = turned(block)

    def mix(step, carry):
        rows = pl.ds(pl.multiple_of(step * QUERY_BLOCK, QUERY_BLOCK), QUERY_BLOCK)
        bias = bias_ref[...]
        for head in range(2):
            span = slice(head * HEAD_DIM, (head + 1) * HEAD_DIM)
            scores = dot(query[rows, span], key[:, span], 1, 1) + bias
            peak = jnp.max(scores, axis=1, keepdims=True)
            expo = jnp.exp(scores - peak)
            expos[head, rows, :] = expo
            share = 1.0 / jnp.sum(expo, axis=1, keepdims=True)
            mixed = dot(expo.astype(BF16), value[:, span], 1, 0) * share
            mixes[rows, span] = mixed
            shares[rows, span] = jnp.broadcast_to(share, (QUERY_BLOCK, HEAD_DIM))
            attended[rows, span] = mixed.astype(BF16)
        return carry

    def attend(which):
        rows = rows_of(which)
        scaled = grad[rows, :].astype(F32) * shares[rows, :]
        scaled_low = scaled.astype(BF16)
        scaled_t = scaled.T.astype(BF16)
        products = mixes[rows, :] * scaled
        for head in range(2):
            span = slice(head * HEAD_DIM, (head + 1) * HEAD_DIM)
            delta = jnp.sum(products[:, span], axis=1, keepdims=True)
            expo = expos[head, rows, :]
            prob_grad = dot(scaled_low[:, span], value[:, span], 1, 1)
            score_grad = (expo * (prob_grad - delta)).astype(BF16)
            grads[rows, span] = (dot(score_grad, key[:, span], 1, 0) * 0.125).astype(BF16)
            key_grad_t[span, :] += dot(query_t[span, rows], score_grad, 1, 0)
            value_grad_t[span, :] += dot(scaled_t[span, :], expo.astype(BF16), 1, 0)

    def back(index, source, target, device):
        return pltpu.make_async_remote_copy(
            src_ref=source,
            dst_ref=target,
            send_sem=back_send.at[index],
            recv_sem=back_recv.at[index],
            device_id={"seq": device},
            device_id_type=MESH,
        )

    def slots(which, columns=slice(0, 384)):
        return grads.at[pl.ds(pl.multiple_of(which * 128, 128), 128), columns]

    first, rest = slice(0, 128), slice(128, 384)

    def send_queries(index, which):
        go(back(index, slots(which, first), returned.at[me, :, first], which))

    def send_rest(index, which):
        go(back(index, slots(which, rest), returned.at[me, :, rest], which))

    across_x, across_y = spot % 4, spot // 4

    def at(step_x, step_y):
        return ((across_y + step_y) % 4) * 4 + (across_x + step_x) % 4

    hops = [(x, y) for y in range(4) for x in range(4) if (x, y) != (0, 0)]

    def scatter(index, source, target, device):
        return pltpu.make_async_remote_copy(
            src_ref=source,
            dst_ref=target,
            send_sem=sum_send.at[index],
            recv_sem=sum_recv.at[index],
            device_id={"dp": device},
            device_id_type=MESH,
        )

    def exchange(base, source, target):
        for x, y in hops:
            to = at(x, y)
            go(scatter(base + y * 4 + x, source.at[:, to], target.at[spot], layer * 16 + to))

    def collect(base, target):
        for x, y in hops:
            view = target.at[at(4 - x, 4 - y)]
            scatter(base + y * 4 + x, view, view, other_layer).wait_recv()

    def add_pieces(own, target):
        summed = own[:, spot].astype(F32)
        for x, y in hops:
            summed = summed + target[at(x, y)].astype(F32)
        return summed

    send_own(0, normed_ref, all_normed)
    for load in loads:
        load.wait()
    out_part[...] = jnp.zeros_like(out_part)
    key_grad_t[...] = jnp.zeros_like(key_grad_t)
    value_grad_t[...] = jnp.zeros_like(value_grad_t)
    relay_first(0, all_normed)
    send_own(13, masked_ref, all_masked)
    relay_second(0, all_normed)
    near_twin(0, all_normed)

    def near_normed(step, carry):
        project_normed((chip + 3 + step) % 4)
        return carry

    lax.fori_loop(0, 3, near_normed, 0)
    relay_far(0, all_normed)
    far_twin_(0, all_normed)
    project_normed(across)
    lax.fori_loop(0, 1024 // QUERY_BLOCK, mix, 0)

    relay_first_fine(13, all_masked)
    relay_second(13, all_masked)
    near_twin(13, all_masked)

    def near_masked(step, carry):
        which = (chip + 3 + step) % 4
        project_masked(which)
        attend(which)
        add_out_terms(which)
        return carry

    lax.fori_loop(0, 3, near_masked, 0)
    send_queries(9, after)
    send_queries(10, after_twin)
    send_queries(11, before)
    send_queries(12, before_twin)
    send_queries(13, mate)
    relay_far_fine(13, all_masked)
    far_twin_fine(13, all_masked)
    project_masked(across)
    attend(across)
    grads[:, 128:256] = key_grad_t[...].T.astype(BF16)
    grads[:, 256:384] = value_grad_t[...].T.astype(BF16)

    go(back(0, slots(far), relayed.at[0], after))
    go(back(1, slots(far_twin), relayed.at[1], before))
    send_rest(2, after)
    send_rest(3, after_twin)
    send_rest(4, before)
    send_rest(5, before_twin)
    send_rest(6, mate)

    pieces[...] = dot(normed_t[...], grads[...], 1, 0).astype(BF16).reshape(2, 4, 4, 32, 384)
    for step in range(1, 4):
        to_x, to_y = (across_x + step) % 4, (across_y + step) % 4
        go(scatter(step, pieces.at[0, :, to_x], row_in.at[across_x], layer * 16 + at(step, 0)))
        go(scatter(step + 3, pieces.at[1, to_y], column_in.at[across_y], layer * 16 + at(0, step)))
    add_out_terms(across)
    out_pieces[...] = out_part[...].astype(BF16).reshape(2, 16, 32, 128)
    exchange(20, out_pieces, out_pieces_in)

    def add_rows(which, block, first=False):
        heads = pl.ds(pl.multiple_of(which * 128, 128), 128)
        term = dot(block[:, :128], weights[0, heads, :], 1, 0)
        term = term + dot(block[:, 128:256], weights[1, heads, :], 1, 0)
        term = term + dot(block[:, 256:], weights[2, heads, :], 1, 0)
        total[...] = term if first else total[...] + term

    def came(index, which, columns=rest):
        view = returned.at[which, :, columns]
        back(index, view, view, mate).wait_recv()

    def came_near(index, which):
        came(index + 7, which, first)
        came(index, which)
        add_rows(which, returned[which])

    add_rows(me, grads[pl.ds(pl.multiple_of(me * 128, 128), 128), :], True)
    came_near(6, mate)
    back(0, relayed.at[0], relayed.at[0], mate).wait_recv()
    go(back(7, relayed.at[0], returned.at[before], after))
    back(1, relayed.at[1], relayed.at[1], mate).wait_recv()
    go(back(8, relayed.at[1], returned.at[after], before_twin))
    row_sum = pieces[0, :, across_x].astype(F32)
    column_sum = pieces[1, across_y].astype(F32)
    for step in range(1, 4):
        from_x, from_y = (across_x + 4 - step) % 4, (across_y + 4 - step) % 4
        view = row_in.at[from_x]
        scatter(step, view, view, other_layer).wait_recv()
        row_sum = row_sum + row_in[from_x].astype(F32)
        view = column_in.at[from_y]
        scatter(step + 3, view, view, other_layer).wait_recv()
        column_sum = column_sum + column_in[from_y].astype(F32)
    row_low[...] = row_sum.astype(BF16)
    column_low[...] = column_sum.astype(BF16)
    for step in range(1, 4):
        to_x, to_y = (across_x + step) % 4, (across_y + step) % 4
        go(scatter(step + 6, row_low.at[to_y], row_end.at[across_y], layer * 16 + at(0, step)))
        go(scatter(step + 9, column_low.at[to_x], column_end.at[across_x], layer * 16 + at(step, 0)))
    came_near(2, before)
    came_near(3, before_twin)

    collect(20, out_pieces_in)
    out_summed = add_pieces(out_pieces, out_pieces_in)
    half_out[:, :, 384:] = out_summed.astype(BF16)
    row_total = row_low[across_y].astype(F32)
    column_total = column_low[across_x].astype(F32)
    for step in range(1, 4):
        from_x, from_y = (across_x + 4 - step) % 4, (across_y + 4 - step) % 4
        view = row_end.at[from_y]
        scatter(step + 6, view, view, other_layer).wait_recv()
        row_total = row_total + row_end[from_y].astype(F32)
        view = column_end.at[from_x]
        scatter(step + 9, view, view, other_layer).wait_recv()
        column_total = column_total + column_end[from_x].astype(F32)
    half_out[0, :, :384] = row_total.astype(BF16)
    half_out[1, :, :384] = column_total.astype(BF16)
    last = scatter(0, half_out.at[1 - layer], half_in, other_layer)
    go(last)
    came_near(4, after)
    came_near(5, after_twin)

    came(7, far, slice(0, 384))
    add_rows(far, returned[far])
    came(8, far_twin, slice(0, 384))
    add_rows(far_twin, returned[far_twin])
    unit_grad = total[...] * gain_ref[...]
    standard = standard_ref[...]
    inner = unit_grad - jnp.mean(unit_grad, axis=1, keepdims=True)
    inner = inner - standard * jnp.mean(unit_grad * standard, axis=1, keepdims=True)
    own_masked = masked_ref[...].reshape(128, 1024).astype(F32)
    d_tokens_ref[...] = (own_masked + inv_ref[...] * inner).astype(BF16)

    last.wait_recv()
    far_half = half_in[...].astype(F32)
    half = jnp.where(layer == 0, row_total, column_total)
    sums_ref[:, :384] = (half + far_half[:, :384]) * factor
    half = jnp.where(layer == 0, out_summed[0], out_summed[1])
    sums_ref[:, 384:] = (half + far_half[:, 384:]) * factor
    for copy in started:
        copy.wait_send()


def place_results(rows_ref, sums_ref, d_tokens_ref, grad_qkv_ref, grad_out_ref):
    d_tokens_ref[...] = rows_ref[...]
    for part in range(3):
        grad_qkv_ref[part] = sums_ref[:, part * 128 : (part + 1) * 128]
    grad_out_ref[...] = sums_ref[:, 384:]


def shards(tokens, positions, counts, ln_gain, w_qkv, w_out, d_out):
    slot_count = tokens.shape[1] * lax.axis_size("seq")
    factor = 1.0 / math.sqrt(lax.axis_size("dp") * (3 * slot_count // 4))
    vmem = pl.BlockSpec(memory_space=pltpu.VMEM)
    anywhere = pl.BlockSpec(memory_space=pl.ANY)
    rows, sums = pl.pallas_call(
        lambda *refs: block_kernel(factor, *refs),
        out_shape=(
            jax.ShapeDtypeStruct((128, 1024), BF16),
            jax.ShapeDtypeStruct((32, 512), F32),
        ),
        in_specs=[
            vmem,
            vmem,
            vmem,
            pl.BlockSpec(memory_space=pltpu.SMEM),
            vmem,
            anywhere,
            anywhere,
        ],
        out_specs=(vmem, vmem),
        scratch_shapes=[
            pltpu.VMEM((2, 64, 1024), BF16),
            pltpu.VMEM((2, 64, 1024), BF16),
            pltpu.VMEM((128, 1024), F32),
            pltpu.VMEM((128, 1), F32),
            pltpu.VMEM((1, 1024), F32),
            pltpu.VMEM((2, 1024, 1024), F32),
            pltpu.VMEM((1024, 128), F32),
            pltpu.VMEM((1024, 128), F32),
            pltpu.VMEM((8, 2, 64, 1024), BF16),
            pltpu.VMEM((8, 2, 64, 1024), BF16),
            pltpu.VMEM((1024, 1024), BF16),
            pltpu.VMEM((1024, 256), BF16),
            pltpu.VMEM((3, 1024, 1024), BF16),
            pltpu.VMEM((1024, 128), BF16),
            pltpu.VMEM((1024, 128), BF16),
            pltpu.VMEM((1024, 128), BF16),
            pltpu.VMEM((1024, 128), BF16),
            pltpu.VMEM((1024, 128), BF16),
            pltpu.VMEM((128, 1024), BF16),
            pltpu.VMEM((128, 1024), F32),
            pltpu.VMEM((128, 1024), F32),
            pltpu.VMEM((1024, 384), BF16),
            pltpu.VMEM((1024, 128), BF16),
            pltpu.VMEM((8, 128, 384), BF16),
            pltpu.VMEM((2, 128, 384), BF16),
            pltpu.VMEM((1024, 128), F32),
            pltpu.VMEM((2, 4, 4, 32, 384), BF16),
            pltpu.VMEM((4, 4, 32, 384), BF16),
            pltpu.VMEM((4, 4, 32, 384), BF16),
            pltpu.VMEM((4, 32, 384), BF16),
            pltpu.VMEM((4, 32, 384), BF16),
            pltpu.VMEM((4, 32, 384), BF16),
            pltpu.VMEM((4, 32, 384), BF16),
            pltpu.VMEM((2, 16, 32, 128), BF16),
            pltpu.VMEM((16, 2, 32, 128), BF16),
            pltpu.VMEM((2, 32, 512), BF16),
            pltpu.VMEM((32, 512), BF16),
            pltpu.VMEM((128, 1024), F32),
            pltpu.SemaphoreType.DMA((2,)),
            pltpu.SemaphoreType.DMA((30,)),
            pltpu.SemaphoreType.DMA((30,)),
            pltpu.SemaphoreType.DMA((14,)),
            pltpu.SemaphoreType.DMA((14,)),
            pltpu.SemaphoreType.DMA((36,)),
            pltpu.SemaphoreType.DMA((36,)),
        ],
        compiler_params=pltpu.CompilerParams(
            collective_id=0, has_side_effects=True, vmem_limit_bytes=60 * 1024 * 1024
        ),
        name="attention_block_grads",
    )(tokens[0], d_out[0], positions, counts, ln_gain[None, :], w_qkv, w_out)
    d_tokens, grad_qkv, grad_out = pl.pallas_call(
        place_results,
        out_shape=(
            jax.ShapeDtypeStruct((128, 1024), BF16),
            jax.ShapeDtypeStruct((3, 32, 128), F32),
            jax.ShapeDtypeStruct((32, 128), F32),
        ),
        in_specs=[vmem] * 2,
        out_specs=(vmem,) * 3,
        name="place_results",
    )(rows, sums)
    return (d_tokens[None], jnp.transpose(grad_qkv, (0, 2, 1)), grad_out)


def solution(mesh):
    placed = (
        P("dp", "seq", None),
        P("dp", "seq"),
        P("dp", None),
        P(),
        P(),
        P(),
        P("dp", "seq", None),
    )
    return jax.shard_map(
        shards,
        mesh=mesh,
        in_specs=placed,
        out_specs=(P("dp", "seq", None), P(None, "seq", "dp"), P("dp", "seq")),
        check_vma=False,
    )
```

```python
import math

import jax
import jax.numpy as jnp
from jax import lax
from jax.experimental import pallas as pl
from jax.experimental.pallas import tpu as pltpu
from jax.sharding import PartitionSpec as P

HEAD_DIM = 64
EPSILON = 1e-06
MASKED = -1e30
F32 = jnp.float32
BF16 = jnp.bfloat16
MESH = pl.DeviceIdType.MESH
QUERY_BLOCK = 256


def sin_cos(angle):
    turns = jnp.floor(angle * (2.0 / math.pi) + 0.5)
    rest = angle - turns * 1.5703125
    rest = rest - turns * 4.837512969970703125e-4
    rest = rest - turns * 7.54978995489188216e-8
    square = rest * rest
    sine = rest + rest * square * (
        -1.6666654611e-1 + square * (8.3321608736e-3 - square * 1.9515295891e-4)
    )
    cosine = (
        1.0
        - 0.5 * square
        + square
        * square
        * (4.166664568298827e-2 + square * (-1.388731625493765e-3 + square * 2.443315711809948e-5))
    )
    quarter = turns - 4.0 * jnp.floor(turns * 0.25)
    odd = (quarter == 1.0) | (quarter == 3.0)
    sine, cosine = jnp.where(odd, cosine, sine), jnp.where(odd, sine, cosine)
    sine = jnp.where(quarter >= 2.0, -sine, sine)
    cosine = jnp.where((quarter == 1.0) | (quarter == 2.0), -cosine, cosine)
    return sine, cosine


def dot(left, right, left_dim, right_dim):
    return lax.dot_general(
        left, right, (((left_dim,), (right_dim,)), ((), ())), preferred_element_type=F32
    )


def turned(block):
    return block.astype(F32).T.astype(BF16)


def block_kernel(
    factor,
    tokens_hbm,
    d_out_hbm,
    positions_ref,
    counts_ref,
    gain_ref,
    w_qkv_ref,
    w_out_ref,
    d_tokens_ref,
    sums_ref,
    tokens_ref,
    d_out_ref,
    normed_ref,
    masked_ref,
    standard_ref,
    inv_ref,
    bias_ref,
    expos,
    mixes,
    shares,
    all_normed,
    all_masked,
    normed_t,
    masked_t,
    weights,
    out_weights,
    query,
    key,
    value,
    grad,
    query_t,
    key_grad_t,
    value_grad_t,
    grads,
    attended,
    returned,
    relayed,
    out_part,
    pieces,
    row_in,
    column_in,
    row_low,
    column_low,
    row_end,
    column_end,
    out_pieces,
    out_pieces_in,
    half_out,
    half_in,
    total,
    load_sem,
    gather_send,
    gather_recv,
    back_send,
    back_recv,
    sum_send,
    sum_recv,
):
    me = lax.axis_index("seq")
    place = lax.axis_index("dp")
    chip, core = me // 2, me % 2
    ahead, behind, across = (chip + 1) % 4, (chip + 3) % 4, (chip + 2) % 4
    twin = 1 - core
    after, before, far, mate = (
        ahead * 2 + core,
        behind * 2 + core,
        across * 2 + core,
        chip * 2 + twin,
    )
    after_twin, before_twin, far_twin = ahead * 2 + twin, behind * 2 + twin, across * 2 + twin
    layer, spot = place // 16, place % 16

    early = [
        pltpu.make_async_copy(tokens_hbm, tokens_ref, load_sem.at[2]),
        pltpu.make_async_copy(d_out_hbm, d_out_ref, load_sem.at[3]),
    ]
    for load in early:
        load.start()
    loads = [
        pltpu.make_async_copy(w_qkv_ref, weights, load_sem.at[0]),
        pltpu.make_async_copy(
            w_out_ref.at[:, pl.ds(pl.multiple_of(me * 128, 128), 128)], out_weights, load_sem.at[1]
        ),
    ]
    barrier = pltpu.get_barrier_semaphore()
    for step in range(1, 8):
        pl.semaphore_signal(
            barrier, inc=1, device_id={"seq": (me + step) % 8}, device_id_type=MESH
        )
    for step in range(1, 16):
        pl.semaphore_signal(
            barrier, inc=1, device_id={"dp": layer * 16 + (spot + step) % 16}, device_id_type=MESH
        )
    other_layer = (1 - layer) * 16 + spot
    pl.semaphore_signal(barrier, inc=1, device_id={"dp": other_layer}, device_id_type=MESH)

    slot = lax.broadcasted_iota(jnp.int32, (1, 128), 1)
    for part in range(8):
        bias_ref[:, part * 128 : (part + 1) * 128] = jnp.where(
            slot < counts_ref[0, part], 0.0, MASKED
        )
    row = lax.broadcasted_iota(jnp.int32, (128, 128), 0)
    lane = lax.broadcasted_iota(jnp.int32, (128, 128), 1)
    places = jnp.sum(
        jnp.where(row == lane, positions_ref[...].astype(F32), 0.0), axis=1, keepdims=True
    )
    freqs = jnp.exp(
        lax.broadcasted_iota(jnp.int32, (1, 512), 1).astype(F32) * (-math.log(10000.0) / 512)
    )
    own_count = counts_ref[0, me]
    for load in early:
        load.wait()
    for load in loads:
        load.start()
    for part in range(4):
        rows = slice(part * 32, (part + 1) * 32)
        sine, cosine = sin_cos(places[rows] * freqs)
        shifted = tokens_ref[rows, :].astype(F32) + jnp.concatenate([sine, cosine], axis=1)
        centred = shifted - jnp.mean(shifted, axis=1, keepdims=True)
        inv_std = lax.rsqrt(jnp.mean(centred * centred, axis=1, keepdims=True) + EPSILON)
        unit = centred * inv_std
        standard_ref[rows, :] = unit
        inv_ref[rows, :] = inv_std
        within = slice((part % 2) * 32, (part % 2) * 32 + 32)
        normed_ref[part // 2, within, :] = (unit * gain_ref[...]).astype(BF16)
        upstream = d_out_ref[rows, :]
        spots = lax.broadcasted_iota(jnp.int32, (32, 1024), 0) + part * 32
        masked_ref[part // 2, within, :] = jnp.where(
            spots < own_count, upstream.astype(F32), 0.0
        ).astype(BF16)
    all_normed[me] = normed_ref[...]
    all_masked[me] = masked_ref[...]
    pl.semaphore_wait(barrier, 23)

    def gather(index, source, target, device):
        return pltpu.make_async_remote_copy(
            src_ref=source,
            dst_ref=target,
            send_sem=gather_send.at[index],
            recv_sem=gather_recv.at[index],
            device_id={"seq": device},
            device_id_type=MESH,
        )

    started = []

    def go(copy):
        copy.start()
        started.append(copy)

    def send_own(base, own, full):
        go(gather(base + 0, own.at[0], full.at[me, 0], after))
        go(gather(base + 1, own.at[1], full.at[me, 1], before))
        go(gather(base + 2, own.at[1], full.at[me, 1], after))
        go(gather(base + 3, own.at[0], full.at[me, 0], before))
        go(gather(base + 4, own, full.at[me], mate))

    def landed(index, full, *spot_):
        view = full.at[spot_]
        gather(index, view, view, mate).wait_recv()

    def relay_first(base, full):
        landed(base + 0, full, before, 0)
        go(gather(base + 5, full.at[before, 0], full.at[before, 0], after))
        go(gather(base + 7, full.at[before, 0], full.at[before, 0], mate))
        landed(base + 1, full, after, 1)
        go(gather(base + 6, full.at[after, 1], full.at[after, 1], before))
        go(gather(base + 8, full.at[after, 1], full.at[after, 1], mate))

    def relay_second(base, full):
        landed(base + 2, full, before, 1)
        go(gather(base + 9, full.at[before, 1], full.at[before, 1], mate))
        landed(base + 3, full, after, 0)
        go(gather(base + 10, full.at[after, 0], full.at[after, 0], mate))

    def relay_far(base, full):
        landed(base + 5, full, far, 0)
        go(gather(base + 11, full.at[far, 0], full.at[far, 0], mate))
        landed(base + 6, full, far, 1)
        go(gather(base + 12, full.at[far, 1], full.at[far, 1], mate))

    upper, lower = slice(0, 32), slice(32, 64)

    def relay_first_fine(base, full):
        landed(base + 0, full, before, 0)
        go(gather(base + 5, full.at[before, 0, upper], full.at[before, 0, upper], after))
        go(gather(26, full.at[before, 0, lower], full.at[before, 0, lower], after))
        go(gather(base + 7, full.at[before, 0], full.at[before, 0], mate))
        landed(base + 1, full, after, 1)
        go(gather(base + 6, full.at[after, 1, upper], full.at[after, 1, upper], before))
        go(gather(27, full.at[after, 1, lower], full.at[after, 1, lower], before))
        go(gather(base + 8, full.at[after, 1], full.at[after, 1], mate))

    def relay_far_fine(base, full):
        landed(base + 5, full, far, 0, upper)
        go(gather(base + 11, full.at[far, 0, upper], full.at[far, 0, upper], mate))
        landed(base + 6, full, far, 1, upper)
        go(gather(base + 12, full.at[far, 1, upper], full.at[far, 1, upper], mate))
        landed(26, full, far, 0, lower)
        go(gather(28, full.at[far, 0, lower], full.at[far, 0, lower], mate))
        landed(27, full, far, 1, lower)
        go(gather(29, full.at[far, 1, lower], full.at[far, 1, lower], mate))

    def far_twin_fine(base, full):
        landed(base + 11, full, far_twin, 0, upper)
        landed(base + 12, full, far_twin, 1, upper)
        landed(28, full, far_twin, 0, lower)
        landed(29, full, far_twin, 1, lower)

    def near_twin(base, full):
        landed(base + 4, full, mate)
        landed(base + 7, full, before_twin, 0)
        landed(base + 8, full, after_twin, 1)
        landed(base + 9, full, before_twin, 1)
        landed(base + 10, full, after_twin, 0)

    def far_twin_(base, full):
        landed(base + 11, full, far_twin, 0)
        landed(base + 12, full, far_twin, 1)

    def rows_of(which):
        return pl.ds(pl.multiple_of(which * 256, 256), 256)

    def project_masked(which):
        rows = rows_of(which)
        block = all_masked[pl.ds(which * 2, 2)].reshape(256, 1024)
        grad[rows, :] = dot(block, out_weights[...], 1, 0).astype(BF16)

    def add_out_terms(which):
        rows = rows_of(which)
        block = all_masked[pl.ds(which * 2, 2)].reshape(256, 1024)
        masked_t[...] = turned(block)
        out_part[...] += dot(masked_t[...], attended[rows, :], 1, 0)

    def project_normed(which):
        rows = rows_of(which)
        block = all_normed[pl.ds(which * 2, 2)].reshape(256, 1024)
        heads = pl.ds(pl.multiple_of(me * 128, 128), 128)
        queries = dot(block, weights[0, heads, :], 1, 1).astype(BF16).astype(F32) * 0.125
        query[rows, :] = queries.astype(BF16)
        query_t[:, rows] = queries.T.astype(BF16)
        key[rows, :] = dot(block, weights[1, heads, :], 1, 1).astype(BF16)
        value[rows, :] = dot(block, weights[2, heads, :], 1, 1).astype(BF16)
        normed_t[:, rows] = turned(block)

    def mix(step, carry):
        rows = pl.ds(pl.multiple_of(step * QUERY_BLOCK, QUERY_BLOCK), QUERY_BLOCK)
        bias = bias_ref[...]
        for head in range(2):
            span = slice(head * HEAD_DIM, (head + 1) * HEAD_DIM)
            scores = dot(query[rows, span], key[:, span], 1, 1) + bias
            peak = jnp.max(scores, axis=1, keepdims=True)
            expo = jnp.exp(scores - peak)
            expos[head, rows, :] = expo
            share = 1.0 / jnp.sum(expo, axis=1, keepdims=True)
            mixed = dot(expo.astype(BF16), value[:, span], 1, 0) * share
            mixes[rows, span] = mixed
            shares[rows, span] = jnp.broadcast_to(share, (QUERY_BLOCK, HEAD_DIM))
            attended[rows, span] = mixed.astype(BF16)
        return carry

    def attend(which):
        rows = rows_of(which)
        scaled = grad[rows, :].astype(F32) * shares[rows, :]
        scaled_low = scaled.astype(BF16)
        scaled_t = scaled.T.astype(BF16)
        products = mixes[rows, :] * scaled
        for head in range(2):
            span = slice(head * HEAD_DIM, (head + 1) * HEAD_DIM)
            delta = jnp.sum(products[:, span], axis=1, keepdims=True)
            expo = expos[head, rows, :]
            prob_grad = dot(scaled_low[:, span], value[:, span], 1, 1)
            score_grad = (expo * (prob_grad - delta)).astype(BF16)
            grads[rows, span] = (dot(score_grad, key[:, span], 1, 0) * 0.125).astype(BF16)
            key_grad_t[span, :] += dot(query_t[span, rows], score_grad, 1, 0)
            value_grad_t[span, :] += dot(scaled_t[span, :], expo.astype(BF16), 1, 0)

    def back(index, source, target, device):
        return pltpu.make_async_remote_copy(
            src_ref=source,
            dst_ref=target,
            send_sem=back_send.at[index],
            recv_sem=back_recv.at[index],
            device_id={"seq": device},
            device_id_type=MESH,
        )

    def slots(which, columns=slice(0, 384)):
        return grads.at[pl.ds(pl.multiple_of(which * 128, 128), 128), columns]

    first, rest = slice(0, 128), slice(128, 384)

    def send_queries(index, which):
        go(back(index, slots(which, first), returned.at[me, :, first], which))

    def send_rest(index, which):
        go(back(index, slots(which, rest), returned.at[me, :, rest], which))

    across_x, across_y = spot % 4, spot // 4

    def at(step_x, step_y):
        return ((across_y + step_y) % 4) * 4 + (across_x + step_x) % 4

    hops = [(x, y) for y in range(4) for x in range(4) if (x, y) != (0, 0)]

    def scatter(index, source, target, device):
        return pltpu.make_async_remote_copy(
            src_ref=source,
            dst_ref=target,
            send_sem=sum_send.at[index],
            recv_sem=sum_recv.at[index],
            device_id={"dp": device},
            device_id_type=MESH,
        )

    def exchange(base, source, target):
        for x, y in hops:
            to = at(x, y)
            go(scatter(base + y * 4 + x, source.at[:, to], target.at[spot], layer * 16 + to))

    def collect(base, target):
        for x, y in hops:
            view = target.at[at(4 - x, 4 - y)]
            scatter(base + y * 4 + x, view, view, other_layer).wait_recv()

    def add_pieces(own, target):
        summed = own[:, spot].astype(F32)
        for x, y in hops:
            summed = summed + target[at(x, y)].astype(F32)
        return summed

    send_own(0, normed_ref, all_normed)
    for load in loads:
        load.wait()
    out_part[...] = jnp.zeros_like(out_part)
    key_grad_t[...] = jnp.zeros_like(key_grad_t)
    value_grad_t[...] = jnp.zeros_like(value_grad_t)
    relay_first(0, all_normed)
    send_own(13, masked_ref, all_masked)
    relay_second(0, all_normed)
    near_twin(0, all_normed)

    def near_normed(step, carry):
        project_normed((chip + 3 + step) % 4)
        return carry

    lax.fori_loop(0, 3, near_normed, 0)
    relay_far(0, all_normed)
    far_twin_(0, all_normed)
    project_normed(across)
    lax.fori_loop(0, 1024 // QUERY_BLOCK, mix, 0)

    relay_first_fine(13, all_masked)
    relay_second(13, all_masked)
    near_twin(13, all_masked)

    def near_masked(step, carry):
        which = (chip + 3 + step) % 4
        project_masked(which)
        attend(which)
        add_out_terms(which)
        return carry

    lax.fori_loop(0, 3, near_masked, 0)
    send_queries(9, after)
    send_queries(10, after_twin)
    send_queries(11, before)
    send_queries(12, before_twin)
    send_queries(13, mate)
    relay_far_fine(13, all_masked)
    far_twin_fine(13, all_masked)
    project_masked(across)
    attend(across)
    grads[:, 128:256] = key_grad_t[...].T.astype(BF16)
    grads[:, 256:384] = value_grad_t[...].T.astype(BF16)

    go(back(0, slots(far), relayed.at[0], after))
    go(back(1, slots(far_twin), relayed.at[1], before))
    send_rest(2, after)
    send_rest(3, after_twin)
    send_rest(4, before)
    send_rest(5, before_twin)
    send_rest(6, mate)

    pieces[...] = dot(normed_t[...], grads[...], 1, 0).astype(BF16).reshape(2, 4, 4, 32, 384)
    for step in range(1, 4):
        to_x, to_y = (across_x + step) % 4, (across_y + step) % 4
        go(scatter(step, pieces.at[0, :, to_x], row_in.at[across_x], layer * 16 + at(step, 0)))
        go(scatter(step + 3, pieces.at[1, to_y], column_in.at[across_y], layer * 16 + at(0, step)))
    add_out_terms(across)
    out_pieces[...] = out_part[...].astype(BF16).reshape(2, 16, 32, 128)
    exchange(20, out_pieces, out_pieces_in)

    def add_rows(which, block, first=False):
        heads = pl.ds(pl.multiple_of(which * 128, 128), 128)
        term = dot(block[:, :128], weights[0, heads, :], 1, 0)
        term = term + dot(block[:, 128:256], weights[1, heads, :], 1, 0)
        term = term + dot(block[:, 256:], weights[2, heads, :], 1, 0)
        total[...] = term if first else total[...] + term

    def came(index, which, columns=rest):
        view = returned.at[which, :, columns]
        back(index, view, view, mate).wait_recv()

    def came_near(index, which):
        came(index + 7, which, first)
        came(index, which)
        add_rows(which, returned[which])

    add_rows(me, grads[pl.ds(pl.multiple_of(me * 128, 128), 128), :], True)
    came_near(6, mate)
    back(0, relayed.at[0], relayed.at[0], mate).wait_recv()
    go(back(7, relayed.at[0], returned.at[before], after))
    back(1, relayed.at[1], relayed.at[1], mate).wait_recv()
    go(back(8, relayed.at[1], returned.at[after], before_twin))
    row_sum = pieces[0, :, across_x].astype(F32)
    column_sum = pieces[1, across_y].astype(F32)
    for step in range(1, 4):
        from_x, from_y = (across_x + 4 - step) % 4, (across_y + 4 - step) % 4
        view = row_in.at[from_x]
        scatter(step, view, view, other_layer).wait_recv()
        row_sum = row_sum + row_in[from_x].astype(F32)
        view = column_in.at[from_y]
        scatter(step + 3, view, view, other_layer).wait_recv()
        column_sum = column_sum + column_in[from_y].astype(F32)
    row_low[...] = row_sum.astype(BF16)
    column_low[...] = column_sum.astype(BF16)
    for step in range(1, 4):
        to_x, to_y = (across_x + step) % 4, (across_y + step) % 4
        go(scatter(step + 6, row_low.at[to_y], row_end.at[across_y], layer * 16 + at(0, step)))
        go(scatter(step + 9, column_low.at[to_x], column_end.at[across_x], layer * 16 + at(step, 0)))
    came_near(2, before)
    came_near(3, before_twin)

    collect(20, out_pieces_in)
    out_summed = add_pieces(out_pieces, out_pieces_in)
    half_out[:, :, 384:] = out_summed.astype(BF16)
    row_total = row_low[across_y].astype(F32)
    column_total = column_low[across_x].astype(F32)
    for step in range(1, 4):
        from_x, from_y = (across_x + 4 - step) % 4, (across_y + 4 - step) % 4
        view = row_end.at[from_y]
        scatter(step + 6, view, view, other_layer).wait_recv()
        row_total = row_total + row_end[from_y].astype(F32)
        view = column_end.at[from_x]
        scatter(step + 9, view, view, other_layer).wait_recv()
        column_total = column_total + column_end[from_x].astype(F32)
    half_out[0, :, :384] = row_total.astype(BF16)
    half_out[1, :, :384] = column_total.astype(BF16)
    last = scatter(0, half_out.at[1 - layer], half_in, other_layer)
    go(last)
    came_near(4, after)
    came_near(5, after_twin)

    came(7, far, slice(0, 384))
    add_rows(far, returned[far])
    came(8, far_twin, slice(0, 384))
    add_rows(far_twin, returned[far_twin])
    unit_grad = total[...] * gain_ref[...]
    standard = standard_ref[...]
    inner = unit_grad - jnp.mean(unit_grad, axis=1, keepdims=True)
    inner = inner - standard * jnp.mean(unit_grad * standard, axis=1, keepdims=True)
    own_masked = masked_ref[...].reshape(128, 1024).astype(F32)
    d_tokens_ref[...] = (own_masked + inv_ref[...] * inner).astype(BF16)

    last.wait_recv()
    far_half = half_in[...].astype(F32)
    half = jnp.where(layer == 0, row_total, column_total)
    sums_ref[:, :384] = (half + far_half[:, :384]) * factor
    half = jnp.where(layer == 0, out_summed[0], out_summed[1])
    sums_ref[:, 384:] = (half + far_half[:, 384:]) * factor
    for copy in started:
        copy.wait_send()


def place_results(rows_ref, sums_ref, d_tokens_ref, grad_qkv_ref, grad_out_ref):
    d_tokens_ref[...] = rows_ref[...]
    for part in range(3):
        grad_qkv_ref[part] = sums_ref[:, part * 128 : (part + 1) * 128]
    grad_out_ref[...] = sums_ref[:, 384:]


def shards(tokens, positions, counts, ln_gain, w_qkv, w_out, d_out):
    slot_count = tokens.shape[1] * lax.axis_size("seq")
    factor = 1.0 / math.sqrt(lax.axis_size("dp") * (3 * slot_count // 4))
    vmem = pl.BlockSpec(memory_space=pltpu.VMEM)
    anywhere = pl.BlockSpec(memory_space=pl.ANY)
    rows, sums = pl.pallas_call(
        lambda *refs: block_kernel(factor, *refs),
        out_shape=(
            jax.ShapeDtypeStruct((128, 1024), BF16),
            jax.ShapeDtypeStruct((32, 512), F32),
        ),
        in_specs=[
            anywhere,
            anywhere,
            vmem,
            pl.BlockSpec(memory_space=pltpu.SMEM),
            vmem,
            anywhere,
            anywhere,
        ],
        out_specs=(vmem, vmem),
        scratch_shapes=[
            pltpu.VMEM((128, 1024), BF16),
            pltpu.VMEM((128, 1024), BF16),
            pltpu.VMEM((2, 64, 1024), BF16),
            pltpu.VMEM((2, 64, 1024), BF16),
            pltpu.VMEM((128, 1024), F32),
            pltpu.VMEM((128, 1), F32),
            pltpu.VMEM((1, 1024), F32),
            pltpu.VMEM((2, 1024, 1024), F32),
            pltpu.VMEM((1024, 128), F32),
            pltpu.VMEM((1024, 128), F32),
            pltpu.VMEM((8, 2, 64, 1024), BF16),
            pltpu.VMEM((8, 2, 64, 1024), BF16),
            pltpu.VMEM((1024, 1024), BF16),
            pltpu.VMEM((1024, 256), BF16),
            pltpu.VMEM((3, 1024, 1024), BF16),
            pltpu.VMEM((1024, 128), BF16),
            pltpu.VMEM((1024, 128), BF16),
            pltpu.VMEM((1024, 128), BF16),
            pltpu.VMEM((1024, 128), BF16),
            pltpu.VMEM((1024, 128), BF16),
            pltpu.VMEM((128, 1024), BF16),
            pltpu.VMEM((128, 1024), F32),
            pltpu.VMEM((128, 1024), F32),
            pltpu.VMEM((1024, 384), BF16),
            pltpu.VMEM((1024, 128), BF16),
            pltpu.VMEM((8, 128, 384), BF16),
            pltpu.VMEM((2, 128, 384), BF16),
            pltpu.VMEM((1024, 128), F32),
            pltpu.VMEM((2, 4, 4, 32, 384), BF16),
            pltpu.VMEM((4, 4, 32, 384), BF16),
            pltpu.VMEM((4, 4, 32, 384), BF16),
            pltpu.VMEM((4, 32, 384), BF16),
            pltpu.VMEM((4, 32, 384), BF16),
            pltpu.VMEM((4, 32, 384), BF16),
            pltpu.VMEM((4, 32, 384), BF16),
            pltpu.VMEM((2, 16, 32, 128), BF16),
            pltpu.VMEM((16, 2, 32, 128), BF16),
            pltpu.VMEM((2, 32, 512), BF16),
            pltpu.VMEM((32, 512), BF16),
            pltpu.VMEM((128, 1024), F32),
            pltpu.SemaphoreType.DMA((4,)),
            pltpu.SemaphoreType.DMA((30,)),
            pltpu.SemaphoreType.DMA((30,)),
            pltpu.SemaphoreType.DMA((14,)),
            pltpu.SemaphoreType.DMA((14,)),
            pltpu.SemaphoreType.DMA((36,)),
            pltpu.SemaphoreType.DMA((36,)),
        ],
        compiler_params=pltpu.CompilerParams(
            collective_id=0, has_side_effects=True, vmem_limit_bytes=60 * 1024 * 1024
        ),
        name="attention_block_grads",
    )(tokens[0], d_out[0], positions, counts, ln_gain[None, :], w_qkv, w_out)
    d_tokens, grad_qkv, grad_out = pl.pallas_call(
        place_results,
        out_shape=(
            jax.ShapeDtypeStruct((128, 1024), BF16),
            jax.ShapeDtypeStruct((3, 32, 128), F32),
            jax.ShapeDtypeStruct((32, 128), F32),
        ),
        in_specs=[vmem] * 2,
        out_specs=(vmem,) * 3,
        name="place_results",
    )(rows, sums)
    return (d_tokens[None], jnp.transpose(grad_qkv, (0, 2, 1)), grad_out)


def solution(mesh):
    placed = (
        P("dp", "seq", None),
        P("dp", "seq"),
        P("dp", None),
        P(),
        P(),
        P(),
        P("dp", "seq", None),
    )
    return jax.shard_map(
        shards,
        mesh=mesh,
        in_specs=placed,
        out_specs=(P("dp", "seq", None), P(None, "seq", "dp"), P("dp", "seq")),
        check_vma=False,
    )
```

```python
import math

import jax
import jax.numpy as jnp
from jax import lax
from jax.experimental import pallas as pl
from jax.experimental.pallas import tpu as pltpu
from jax.sharding import PartitionSpec as P

HEAD_DIM = 64
EPSILON = 1e-06
MASKED = -1e30
F32 = jnp.float32
BF16 = jnp.bfloat16
MESH = pl.DeviceIdType.MESH
QUERY_BLOCK = 256


def sin_cos(angle):
    turns = jnp.floor(angle * (2.0 / math.pi) + 0.5)
    rest = angle - turns * 1.5703125
    rest = rest - turns * 4.837512969970703125e-4
    rest = rest - turns * 7.54978995489188216e-8
    square = rest * rest
    sine = rest + rest * square * (
        -1.6666654611e-1 + square * (8.3321608736e-3 - square * 1.9515295891e-4)
    )
    cosine = (
        1.0
        - 0.5 * square
        + square
        * square
        * (4.166664568298827e-2 + square * (-1.388731625493765e-3 + square * 2.443315711809948e-5))
    )
    quarter = turns - 4.0 * jnp.floor(turns * 0.25)
    odd = (quarter == 1.0) | (quarter == 3.0)
    sine, cosine = jnp.where(odd, cosine, sine), jnp.where(odd, sine, cosine)
    sine = jnp.where(quarter >= 2.0, -sine, sine)
    cosine = jnp.where((quarter == 1.0) | (quarter == 2.0), -cosine, cosine)
    return sine, cosine


def dot(left, right, left_dim, right_dim):
    return lax.dot_general(
        left, right, (((left_dim,), (right_dim,)), ((), ())), preferred_element_type=F32
    )


def turned(block):
    return block.astype(F32).T.astype(BF16)


def block_kernel(
    factor,
    tokens_hbm,
    d_out_hbm,
    positions_ref,
    counts_ref,
    gain_ref,
    w_qkv_ref,
    w_out_ref,
    d_tokens_ref,
    sums_ref,
    tokens_ref,
    d_out_ref,
    normed_ref,
    masked_ref,
    standard_ref,
    inv_ref,
    bias_ref,
    expos,
    mixes,
    shares,
    all_normed,
    all_masked,
    normed_t,
    masked_t,
    weights,
    out_weights,
    query,
    key,
    value,
    grad,
    query_t,
    key_grad_t,
    value_grad_t,
    grads,
    attended,
    returned,
    relayed,
    out_part,
    pieces,
    row_in,
    column_in,
    row_low,
    column_low,
    row_end,
    column_end,
    out_pieces,
    out_pieces_in,
    half_out,
    half_in,
    total,
    load_sem,
    gather_send,
    gather_recv,
    back_send,
    back_recv,
    sum_send,
    sum_recv,
):
    me = lax.axis_index("seq")
    place = lax.axis_index("dp")
    chip, core = me // 2, me % 2
    ahead, behind, across = (chip + 1) % 4, (chip + 3) % 4, (chip + 2) % 4
    twin = 1 - core
    after, before, far, mate = (
        ahead * 2 + core,
        behind * 2 + core,
        across * 2 + core,
        chip * 2 + twin,
    )
    after_twin, before_twin, far_twin = ahead * 2 + twin, behind * 2 + twin, across * 2 + twin
    layer, spot = place // 16, place % 16

    early = [
        pltpu.make_async_copy(tokens_hbm, tokens_ref, load_sem.at[2]),
        pltpu.make_async_copy(d_out_hbm, d_out_ref, load_sem.at[3]),
    ]
    for load in early:
        load.start()
    loads = [
        pltpu.make_async_copy(w_qkv_ref, weights, load_sem.at[0]),
        pltpu.make_async_copy(
            w_out_ref.at[:, pl.ds(pl.multiple_of(me * 128, 128), 128)], out_weights, load_sem.at[1]
        ),
    ]
    barrier = pltpu.get_barrier_semaphore()
    for step in range(1, 8):
        pl.semaphore_signal(
            barrier, inc=1, device_id={"seq": (me + step) % 8}, device_id_type=MESH
        )
    for step in range(1, 16):
        pl.semaphore_signal(
            barrier, inc=1, device_id={"dp": layer * 16 + (spot + step) % 16}, device_id_type=MESH
        )
    other_layer = (1 - layer) * 16 + spot
    pl.semaphore_signal(barrier, inc=1, device_id={"dp": other_layer}, device_id_type=MESH)

    slot = lax.broadcasted_iota(jnp.int32, (1, 128), 1)
    for part in range(8):
        bias_ref[:, part * 128 : (part + 1) * 128] = jnp.where(
            slot < counts_ref[0, part], 0.0, MASKED
        )
    row = lax.broadcasted_iota(jnp.int32, (128, 128), 0)
    lane = lax.broadcasted_iota(jnp.int32, (128, 128), 1)
    places = jnp.sum(
        jnp.where(row == lane, positions_ref[...].astype(F32), 0.0), axis=1, keepdims=True
    )
    freqs = jnp.exp(
        lax.broadcasted_iota(jnp.int32, (1, 512), 1).astype(F32) * (-math.log(10000.0) / 512)
    )
    own_count = counts_ref[0, me]
    for load in early:
        load.wait()
    for load in loads:
        load.start()
    for part in range(4):
        rows = slice(part * 32, (part + 1) * 32)
        sine, cosine = sin_cos(places[rows] * freqs)
        shifted = tokens_ref[rows, :].astype(F32) + jnp.concatenate([sine, cosine], axis=1)
        centred = shifted - jnp.mean(shifted, axis=1, keepdims=True)
        inv_std = lax.rsqrt(jnp.mean(centred * centred, axis=1, keepdims=True) + EPSILON)
        unit = centred * inv_std
        standard_ref[rows, :] = unit
        inv_ref[rows, :] = inv_std
        within = slice((part % 2) * 32, (part % 2) * 32 + 32)
        normed_ref[part // 2, within, :] = (unit * gain_ref[...]).astype(BF16)
        upstream = d_out_ref[rows, :]
        spots = lax.broadcasted_iota(jnp.int32, (32, 1024), 0) + part * 32
        masked_ref[part // 2, within, :] = jnp.where(
            spots < own_count, upstream.astype(F32), 0.0
        ).astype(BF16)
    all_normed[me] = normed_ref[...]
    all_masked[me] = masked_ref[...]
    pl.semaphore_wait(barrier, 23)

    def gather(index, source, target, device):
        return pltpu.make_async_remote_copy(
            src_ref=source,
            dst_ref=target,
            send_sem=gather_send.at[index],
            recv_sem=gather_recv.at[index],
            device_id={"seq": device},
            device_id_type=MESH,
        )

    started = []

    def go(copy):
        copy.start()
        started.append(copy)

    def send_own(base, own, full):
        go(gather(base + 0, own.at[0], full.at[me, 0], after))
        go(gather(base + 1, own.at[1], full.at[me, 1], before))
        go(gather(base + 2, own.at[1], full.at[me, 1], after))
        go(gather(base + 3, own.at[0], full.at[me, 0], before))
        go(gather(base + 4, own, full.at[me], mate))

    def landed(index, full, *spot_):
        view = full.at[spot_]
        gather(index, view, view, mate).wait_recv()

    def relay_first(base, full):
        landed(base + 0, full, before, 0)
        go(gather(base + 5, full.at[before, 0], full.at[before, 0], after))
        go(gather(base + 7, full.at[before, 0], full.at[before, 0], mate))
        landed(base + 1, full, after, 1)
        go(gather(base + 6, full.at[after, 1], full.at[after, 1], before))
        go(gather(base + 8, full.at[after, 1], full.at[after, 1], mate))

    def relay_second(base, full):
        landed(base + 2, full, before, 1)
        go(gather(base + 9, full.at[before, 1], full.at[before, 1], mate))
        landed(base + 3, full, after, 0)
        go(gather(base + 10, full.at[after, 0], full.at[after, 0], mate))

    def relay_far(base, full):
        landed(base + 5, full, far, 0)
        go(gather(base + 11, full.at[far, 0], full.at[far, 0], mate))
        landed(base + 6, full, far, 1)
        go(gather(base + 12, full.at[far, 1], full.at[far, 1], mate))

    upper, lower = slice(0, 32), slice(32, 64)

    def relay_first_fine(base, full):
        landed(base + 0, full, before, 0)
        go(gather(base + 5, full.at[before, 0, upper], full.at[before, 0, upper], after))
        go(gather(26, full.at[before, 0, lower], full.at[before, 0, lower], after))
        go(gather(base + 7, full.at[before, 0], full.at[before, 0], mate))
        landed(base + 1, full, after, 1)
        go(gather(base + 6, full.at[after, 1, upper], full.at[after, 1, upper], before))
        go(gather(27, full.at[after, 1, lower], full.at[after, 1, lower], before))
        go(gather(base + 8, full.at[after, 1], full.at[after, 1], mate))

    def relay_far_fine(base, full):
        landed(base + 5, full, far, 0, upper)
        go(gather(base + 11, full.at[far, 0, upper], full.at[far, 0, upper], mate))
        landed(base + 6, full, far, 1, upper)
        go(gather(base + 12, full.at[far, 1, upper], full.at[far, 1, upper], mate))
        landed(26, full, far, 0, lower)
        go(gather(28, full.at[far, 0, lower], full.at[far, 0, lower], mate))
        landed(27, full, far, 1, lower)
        go(gather(29, full.at[far, 1, lower], full.at[far, 1, lower], mate))

    def far_twin_fine(base, full):
        landed(base + 11, full, far_twin, 0, upper)
        landed(base + 12, full, far_twin, 1, upper)
        landed(28, full, far_twin, 0, lower)
        landed(29, full, far_twin, 1, lower)

    def near_twin(base, full):
        landed(base + 4, full, mate)
        landed(base + 7, full, before_twin, 0)
        landed(base + 8, full, after_twin, 1)
        landed(base + 9, full, before_twin, 1)
        landed(base + 10, full, after_twin, 0)

    def far_twin_(base, full):
        landed(base + 11, full, far_twin, 0)
        landed(base + 12, full, far_twin, 1)

    def rows_of(which):
        return pl.ds(pl.multiple_of(which * 256, 256), 256)

    def project_masked(which):
        rows = rows_of(which)
        block = all_masked[pl.ds(which * 2, 2)].reshape(256, 1024)
        grad[rows, :] = dot(block, out_weights[...], 1, 0).astype(BF16)

    def add_out_terms(which):
        rows = rows_of(which)
        block = all_masked[pl.ds(which * 2, 2)].reshape(256, 1024)
        masked_t[...] = turned(block)
        out_part[...] += dot(masked_t[...], attended[rows, :], 1, 0)

    def project_normed(which):
        rows = rows_of(which)
        block = all_normed[pl.ds(which * 2, 2)].reshape(256, 1024)
        heads = pl.ds(pl.multiple_of(me * 128, 128), 128)
        queries = dot(block, weights[0, heads, :], 1, 1).astype(BF16).astype(F32) * 0.125
        query[rows, :] = queries.astype(BF16)
        query_t[:, rows] = queries.T.astype(BF16)
        key[rows, :] = dot(block, weights[1, heads, :], 1, 1).astype(BF16)
        value[rows, :] = dot(block, weights[2, heads, :], 1, 1).astype(BF16)
        normed_t[:, rows] = turned(block)

    def mix(step, carry):
        rows = pl.ds(pl.multiple_of(step * QUERY_BLOCK, QUERY_BLOCK), QUERY_BLOCK)
        bias = bias_ref[...]
        for head in range(2):
            span = slice(head * HEAD_DIM, (head + 1) * HEAD_DIM)
            scores = dot(query[rows, span], key[:, span], 1, 1) + bias
            peak = jnp.max(scores, axis=1, keepdims=True)
            expo = jnp.exp(scores - peak)
            expos[head, rows, :] = expo
            share = 1.0 / jnp.sum(expo, axis=1, keepdims=True)
            mixed = dot(expo.astype(BF16), value[:, span], 1, 0) * share
            mixes[rows, span] = mixed
            shares[rows, span] = jnp.broadcast_to(share, (QUERY_BLOCK, HEAD_DIM))
            attended[rows, span] = mixed.astype(BF16)
        return carry

    def attend(which):
        rows = rows_of(which)
        scaled = grad[rows, :].astype(F32) * shares[rows, :]
        scaled_low = scaled.astype(BF16)
        scaled_t = scaled.T.astype(BF16)
        products = mixes[rows, :] * scaled
        for head in range(2):
            span = slice(head * HEAD_DIM, (head + 1) * HEAD_DIM)
            delta = jnp.sum(products[:, span], axis=1, keepdims=True)
            expo = expos[head, rows, :]
            prob_grad = dot(scaled_low[:, span], value[:, span], 1, 1)
            score_grad = (expo * (prob_grad - delta)).astype(BF16)
            grads[rows, span] = (dot(score_grad, key[:, span], 1, 0) * 0.125).astype(BF16)
            key_grad_t[span, :] += dot(query_t[span, rows], score_grad, 1, 0)
            value_grad_t[span, :] += dot(scaled_t[span, :], expo.astype(BF16), 1, 0)

    def back(index, source, target, device):
        return pltpu.make_async_remote_copy(
            src_ref=source,
            dst_ref=target,
            send_sem=back_send.at[index],
            recv_sem=back_recv.at[index],
            device_id={"seq": device},
            device_id_type=MESH,
        )

    def slots(which, columns=slice(0, 384)):
        return grads.at[pl.ds(pl.multiple_of(which * 128, 128), 128), columns]

    first, rest = slice(0, 128), slice(128, 384)

    def send_queries(index, which):
        go(back(index, slots(which, first), returned.at[me, :, first], which))

    def send_rest(index, which):
        go(back(index, slots(which, rest), returned.at[me, :, rest], which))

    across_x, across_y = spot % 4, spot // 4

    def at(step_x, step_y):
        return ((across_y + step_y) % 4) * 4 + (across_x + step_x) % 4

    hops = [(x, y) for y in range(4) for x in range(4) if (x, y) != (0, 0)]

    def scatter(index, source, target, device):
        return pltpu.make_async_remote_copy(
            src_ref=source,
            dst_ref=target,
            send_sem=sum_send.at[index],
            recv_sem=sum_recv.at[index],
            device_id={"dp": device},
            device_id_type=MESH,
        )

    def exchange(base, source, target):
        for x, y in hops:
            to = at(x, y)
            go(scatter(base + y * 4 + x, source.at[:, to], target.at[spot], layer * 16 + to))

    def collect(base, target):
        for x, y in hops:
            view = target.at[at(4 - x, 4 - y)]
            scatter(base + y * 4 + x, view, view, other_layer).wait_recv()

    def add_pieces(own, target):
        summed = own[:, spot].astype(F32)
        for x, y in hops:
            summed = summed + target[at(x, y)].astype(F32)
        return summed

    send_own(0, normed_ref, all_normed)
    for load in loads:
        load.wait()
    out_part[...] = jnp.zeros_like(out_part)
    key_grad_t[...] = jnp.zeros_like(key_grad_t)
    value_grad_t[...] = jnp.zeros_like(value_grad_t)
    relay_first(0, all_normed)
    send_own(13, masked_ref, all_masked)
    relay_second(0, all_normed)
    near_twin(0, all_normed)

    def near_normed(step, carry):
        project_normed((chip + 3 + step) % 4)
        return carry

    lax.fori_loop(0, 3, near_normed, 0)
    relay_far(0, all_normed)
    far_twin_(0, all_normed)
    project_normed(across)
    lax.fori_loop(0, 1024 // QUERY_BLOCK, mix, 0)

    relay_first_fine(13, all_masked)
    relay_second(13, all_masked)
    near_twin(13, all_masked)

    def near_masked(step, carry):
        which = (chip + 3 + step) % 4
        project_masked(which)
        attend(which)
        add_out_terms(which)
        return carry

    lax.fori_loop(0, 3, near_masked, 0)
    send_queries(9, after)
    send_queries(10, after_twin)
    send_queries(11, before)
    send_queries(12, before_twin)
    send_queries(13, mate)
    relay_far_fine(13, all_masked)
    far_twin_fine(13, all_masked)
    project_masked(across)
    attend(across)
    grads[:, 128:256] = key_grad_t[...].T.astype(BF16)
    grads[:, 256:384] = value_grad_t[...].T.astype(BF16)

    go(back(0, slots(far), relayed.at[0], after))
    go(back(1, slots(far_twin), relayed.at[1], before))
    send_rest(2, after)
    send_rest(3, after_twin)
    send_rest(4, before)
    send_rest(5, before_twin)
    send_rest(6, mate)

    pieces[...] = dot(normed_t[...], grads[...], 1, 0).astype(BF16).reshape(2, 4, 4, 32, 384)
    for step in range(1, 4):
        to_x, to_y = (across_x + step) % 4, (across_y + step) % 4
        go(scatter(step, pieces.at[0, :, to_x], row_in.at[across_x], layer * 16 + at(step, 0)))
        go(scatter(step + 3, pieces.at[1, to_y], column_in.at[across_y], layer * 16 + at(0, step)))
    add_out_terms(across)
    out_pieces[...] = out_part[...].astype(BF16).reshape(2, 16, 32, 128)
    exchange(20, out_pieces, out_pieces_in)

    def add_rows(which, block, first=False):
        heads = pl.ds(pl.multiple_of(which * 128, 128), 128)
        term = dot(block, weights[:, heads, :].reshape(384, 1024), 1, 0)
        total[...] = term if first else total[...] + term

    def came(index, which, columns=rest):
        view = returned.at[which, :, columns]
        back(index, view, view, mate).wait_recv()

    def came_near(index, which):
        came(index + 7, which, first)
        came(index, which)
        add_rows(which, returned[which])

    add_rows(me, grads[pl.ds(pl.multiple_of(me * 128, 128), 128), :], True)
    came_near(6, mate)
    back(0, relayed.at[0], relayed.at[0], mate).wait_recv()
    go(back(7, relayed.at[0], returned.at[before], after))
    back(1, relayed.at[1], relayed.at[1], mate).wait_recv()
    go(back(8, relayed.at[1], returned.at[after], before_twin))
    row_sum = pieces[0, :, across_x].astype(F32)
    column_sum = pieces[1, across_y].astype(F32)
    for step in range(1, 4):
        from_x, from_y = (across_x + 4 - step) % 4, (across_y + 4 - step) % 4
        view = row_in.at[from_x]
        scatter(step, view, view, other_layer).wait_recv()
        row_sum = row_sum + row_in[from_x].astype(F32)
        view = column_in.at[from_y]
        scatter(step + 3, view, view, other_layer).wait_recv()
        column_sum = column_sum + column_in[from_y].astype(F32)
    row_low[...] = row_sum.astype(BF16)
    column_low[...] = column_sum.astype(BF16)
    for step in range(1, 4):
        to_x, to_y = (across_x + step) % 4, (across_y + step) % 4
        go(scatter(step + 6, row_low.at[to_y], row_end.at[across_y], layer * 16 + at(0, step)))
        go(scatter(step + 9, column_low.at[to_x], column_end.at[across_x], layer * 16 + at(step, 0)))
    came_near(2, before)
    came_near(3, before_twin)

    collect(20, out_pieces_in)
    out_summed = add_pieces(out_pieces, out_pieces_in)
    half_out[:, :, 384:] = out_summed.astype(BF16)
    row_total = row_low[across_y].astype(F32)
    column_total = column_low[across_x].astype(F32)
    for step in range(1, 4):
        from_x, from_y = (across_x + 4 - step) % 4, (across_y + 4 - step) % 4
        view = row_end.at[from_y]
        scatter(step + 6, view, view, other_layer).wait_recv()
        row_total = row_total + row_end[from_y].astype(F32)
        view = column_end.at[from_x]
        scatter(step + 9, view, view, other_layer).wait_recv()
        column_total = column_total + column_end[from_x].astype(F32)
    half_out[0, :, :384] = row_total.astype(BF16)
    half_out[1, :, :384] = column_total.astype(BF16)
    last = scatter(0, half_out.at[1 - layer], half_in, other_layer)
    go(last)
    came_near(4, after)
    came_near(5, after_twin)

    came(7, far, slice(0, 384))
    add_rows(far, returned[far])
    came(8, far_twin, slice(0, 384))
    add_rows(far_twin, returned[far_twin])
    unit_grad = total[...] * gain_ref[...]
    standard = standard_ref[...]
    inner = unit_grad - jnp.mean(unit_grad, axis=1, keepdims=True)
    inner = inner - standard * jnp.mean(unit_grad * standard, axis=1, keepdims=True)
    own_masked = masked_ref[...].reshape(128, 1024).astype(F32)
    d_tokens_ref[...] = (own_masked + inv_ref[...] * inner).astype(BF16)

    last.wait_recv()
    far_half = half_in[...].astype(F32)
    half = jnp.where(layer == 0, row_total, column_total)
    sums_ref[:, :384] = (half + far_half[:, :384]) * factor
    half = jnp.where(layer == 0, out_summed[0], out_summed[1])
    sums_ref[:, 384:] = (half + far_half[:, 384:]) * factor
    for copy in started:
        copy.wait_send()


def place_results(rows_ref, sums_ref, d_tokens_ref, grad_qkv_ref, grad_out_ref):
    d_tokens_ref[...] = rows_ref[...]
    for part in range(3):
        grad_qkv_ref[part] = sums_ref[:, part * 128 : (part + 1) * 128]
    grad_out_ref[...] = sums_ref[:, 384:]


def shards(tokens, positions, counts, ln_gain, w_qkv, w_out, d_out):
    slot_count = tokens.shape[1] * lax.axis_size("seq")
    factor = 1.0 / math.sqrt(lax.axis_size("dp") * (3 * slot_count // 4))
    vmem = pl.BlockSpec(memory_space=pltpu.VMEM)
    anywhere = pl.BlockSpec(memory_space=pl.ANY)
    rows, sums = pl.pallas_call(
        lambda *refs: block_kernel(factor, *refs),
        out_shape=(
            jax.ShapeDtypeStruct((128, 1024), BF16),
            jax.ShapeDtypeStruct((32, 512), F32),
        ),
        in_specs=[
            anywhere,
            anywhere,
            vmem,
            pl.BlockSpec(memory_space=pltpu.SMEM),
            vmem,
            anywhere,
            anywhere,
        ],
        out_specs=(vmem, vmem),
        scratch_shapes=[
            pltpu.VMEM((128, 1024), BF16),
            pltpu.VMEM((128, 1024), BF16),
            pltpu.VMEM((2, 64, 1024), BF16),
            pltpu.VMEM((2, 64, 1024), BF16),
            pltpu.VMEM((128, 1024), F32),
            pltpu.VMEM((128, 1), F32),
            pltpu.VMEM((1, 1024), F32),
            pltpu.VMEM((2, 1024, 1024), F32),
            pltpu.VMEM((1024, 128), F32),
            pltpu.VMEM((1024, 128), F32),
            pltpu.VMEM((8, 2, 64, 1024), BF16),
            pltpu.VMEM((8, 2, 64, 1024), BF16),
            pltpu.VMEM((1024, 1024), BF16),
            pltpu.VMEM((1024, 256), BF16),
            pltpu.VMEM((3, 1024, 1024), BF16),
            pltpu.VMEM((1024, 128), BF16),
            pltpu.VMEM((1024, 128), BF16),
            pltpu.VMEM((1024, 128), BF16),
            pltpu.VMEM((1024, 128), BF16),
            pltpu.VMEM((1024, 128), BF16),
            pltpu.VMEM((128, 1024), BF16),
            pltpu.VMEM((128, 1024), F32),
            pltpu.VMEM((128, 1024), F32),
            pltpu.VMEM((1024, 384), BF16),
            pltpu.VMEM((1024, 128), BF16),
            pltpu.VMEM((8, 128, 384), BF16),
            pltpu.VMEM((2, 128, 384), BF16),
            pltpu.VMEM((1024, 128), F32),
            pltpu.VMEM((2, 4, 4, 32, 384), BF16),
            pltpu.VMEM((4, 4, 32, 384), BF16),
            pltpu.VMEM((4, 4, 32, 384), BF16),
            pltpu.VMEM((4, 32, 384), BF16),
            pltpu.VMEM((4, 32, 384), BF16),
            pltpu.VMEM((4, 32, 384), BF16),
            pltpu.VMEM((4, 32, 384), BF16),
            pltpu.VMEM((2, 16, 32, 128), BF16),
            pltpu.VMEM((16, 2, 32, 128), BF16),
            pltpu.VMEM((2, 32, 512), BF16),
            pltpu.VMEM((32, 512), BF16),
            pltpu.VMEM((128, 1024), F32),
            pltpu.SemaphoreType.DMA((4,)),
            pltpu.SemaphoreType.DMA((30,)),
            pltpu.SemaphoreType.DMA((30,)),
            pltpu.SemaphoreType.DMA((14,)),
            pltpu.SemaphoreType.DMA((14,)),
            pltpu.SemaphoreType.DMA((36,)),
            pltpu.SemaphoreType.DMA((36,)),
        ],
        compiler_params=pltpu.CompilerParams(
            collective_id=0, has_side_effects=True, vmem_limit_bytes=60 * 1024 * 1024
        ),
        name="attention_block_grads",
    )(tokens[0], d_out[0], positions, counts, ln_gain[None, :], w_qkv, w_out)
    d_tokens, grad_qkv, grad_out = pl.pallas_call(
        place_results,
        out_shape=(
            jax.ShapeDtypeStruct((128, 1024), BF16),
            jax.ShapeDtypeStruct((3, 32, 128), F32),
            jax.ShapeDtypeStruct((32, 128), F32),
        ),
        in_specs=[vmem] * 2,
        out_specs=(vmem,) * 3,
        name="place_results",
    )(rows, sums)
    return (d_tokens[None], jnp.transpose(grad_qkv, (0, 2, 1)), grad_out)


def solution(mesh):
    placed = (
        P("dp", "seq", None),
        P("dp", "seq"),
        P("dp", None),
        P(),
        P(),
        P(),
        P("dp", "seq", None),
    )
    return jax.shard_map(
        shards,
        mesh=mesh,
        in_specs=placed,
        out_specs=(P("dp", "seq", None), P(None, "seq", "dp"), P("dp", "seq")),
        check_vma=False,
    )
```
